32 devices in a mesh: facet: 8 (over z, y), col: 4 (over x, core).
Axes of the slice: x: 2, y: 2, z: 4, core: 2. Of those that a mesh axis runs over, the one named last changes fastest.
Arguments:
- strip: bfloat16 [2, 64, 32768], P(None, None, 'facet'), may hold values from -6 to 6
- screen_first: bfloat16 [2, 512, 512], replicated, may hold values from -1 to 1
- screen_second: bfloat16 [2, 512, 512], replicated, may hold values from -1 to 1
- owners: int32 [4, 512, 3], P('col', 'facet'), may hold values from 0 to 15, all different within a row; in each aligned block of 64 rows (0 to 63, 64 to 127, ..., all dimensions but the last counted through in order) at most 14 rows name the same one
- live: int32 [4, 512, 3], P('col', 'facet'), may hold values 0 or 1
- place: int32 [4, 512, 3], P('col', 'facet'), may hold values from 0 to 63
Outputs:
- facet_image: float32 [2, 64, 32768], P(None, None, ('facet', 'col'))
The draws below stay inside these ranges and needn't reach their ends.
Inputs may be any that keep to these rules, and one draw needn't show every extreme that they name: `owners`: each row names three different subgrids; among the rows of one device no subgrid is named more than 14 times, a bound that some block reaches. `place`: tile p lies at tile row p // 8 and tile column p % 8.
All inputs are finite; a program needn't handle non-finite values. No bound on the sum of `live` on one device may be relied on, other than what follows from the above.
Results may differ from the reference program's by a relative error of at most 0.013.
Values may be sent and summed in bfloat16 or wider, within the bound.
A program may use at most 64 MiB of HBM per device.

```python
import math
import jax
import jax.numpy as jnp
import numpy as np
from jax import lax

WIN = 64
SUB = 512
WIN_DEV = 64
POS = 64
WINDOWS = 512
SUBGRIDS = 16
COLS = 4
CAP = 14
N_COL = 4


def place_ends(drawn, stream_key, least, high):
    extent = drawn.shape
    index_at = [jax.random.randint(jax.random.fold_in(stream_key, axis), (), 0, extent[axis]) for axis in range(len(extent))]
    drawn = drawn.at[tuple(index_at)].set(least)
    longest = extent.index(max(extent))
    index_at[longest] = (index_at[longest] + 1) % extent[longest]
    return drawn.at[tuple(index_at)].set(high)


def shard_levels(own_key, shape, shards, low, top_value):
    gain = 1.0
    for position, shards_of in shards:
        steps = jax.random.uniform(jax.random.fold_in(jax.random.fold_in(own_key, 6), position), (shards_of,), jnp.float32, low / len(shards), top_value / len(shards))
        gain = gain * jnp.repeat(jnp.exp(steps), shape[position] // shards_of).reshape((-1,) + (1,) * (len(shape) - 1 - position))
    return gain


def deal_out(key, own, number, rows, count, top, limit, slope):
    ranking = jax.random.permutation(key, count)
    crowded, usual = load_shares(count, rows * top, limit, slope, True), load_shares(count, rows * top, limit, slope, False)
    places = jnp.arange(count)

    def named(lengths, offset_by):
        used = int((lengths > 0).sum())
        fixed = max(1, used // 4)
        moved = fixed + (places - fixed + offset_by * (used - fixed)) % max(1, count - fixed)
        return jnp.zeros((count,), jnp.int32).at[ranking[jnp.where(places < fixed, places, moved)]].set(jnp.asarray(lengths, jnp.int32))

    lengths = jnp.where(number % 4 == 0, named(crowded, number // 4), named(usual, number - number // 4 - 1))
    mixed = jax.random.permutation(jax.random.fold_in(own, 3), count)
    source_of, receiver = mixed[0:count // 2 * 2:2], mixed[1:count // 2 * 2:2]
    slack = jnp.minimum(lengths[source_of] - 1, limit - lengths[receiver]) // 2
    slack = jnp.where((source_of == ranking[0]) | (receiver == ranking[0]) | (lengths[receiver] == 0), 0, jnp.maximum(slack, 0))
    moved = jax.random.randint(jax.random.fold_in(own, 4), (count // 2,), 0, 1 << 20) % (slack + 1)
    lengths = lengths.at[source_of].add(-moved).at[receiver].add(moved)
    members = jnp.searchsorted(jnp.cumsum(lengths), jnp.arange(rows * top), side="right").astype(jnp.int32)
    table = members.reshape(top, rows).T
    table = table[jax.random.permutation(jax.random.fold_in(own, 1), rows)]
    offset_by = jax.random.randint(jax.random.fold_in(own, 2), (rows, 1), 0, top)
    return jnp.take_along_axis(table, (jnp.arange(top)[None, :] + offset_by) % top, axis=1)


def load_shares(amount, total, most, skew, full):
    portions = [(1 << 20) // math.isqrt(standing ** skew) + 1 for standing in range(1, amount + 1)]
    largest = most if full else min(most, max(-(-total // amount), total * portions[0] // sum(portions)))
    least = 1 if total - largest >= amount - 1 else 0
    counts, rest = [largest] + [least] * (amount - 1), total - largest - least * (amount - 1)
    while rest > 0:
        candidates = [i for i in range(1, amount) if counts[i] < largest] or [i for i in range(1, amount) if counts[i] < most]
        mass, remaining = sum([portions[i] for i in candidates]), rest
        for i in candidates:
            extra = min(most - counts[i], max(1, remaining * portions[i] // mass), rest)
            counts[i] = counts[i] + extra
            rest = rest - extra
    return np.array(counts)


def scatter_about(own_key, dims, deviation, limit, split=(), kind=jnp.bfloat16):
    entries = jax.random.normal(own_key, dims, jnp.float32) * deviation
    if len(split) > 0:
        entries = shard_levels(own_key, dims, split, -0.22, 0.18) * entries
    return jnp.clip(entries, min=-limit, max=limit).astype(kind)


def setup_inputs(seed: int = 0) -> dict:
    splits = jax.random.split(jax.random.key(seed), 7)
    strip = scatter_about(splits[0], (2, WIN, WINDOWS * WIN), 1.0, 6.0, ((2, 8),))
    screen_first = jnp.clip(jax.random.uniform(splits[1], (2, SUB, SUB), jnp.float32, -1.0, 1.0), -1.0, 1.0).astype(jnp.bfloat16)
    screen_second = jnp.clip(jax.random.uniform(splits[2], (2, SUB, SUB), jnp.float32, -1.0, 1.0), -1.0, 1.0).astype(jnp.bfloat16)
    owners_keys = jax.random.split(jax.random.fold_in(splits[3], 1), COLS * WINDOWS // WIN_DEV)
    owners_turns = jax.random.permutation(jax.random.fold_in(splits[3], 3), COLS * WINDOWS // WIN_DEV)
    owners = jax.vmap(lambda own, number: deal_out(jax.random.fold_in(splits[3], 2), own, number, WIN_DEV, SUBGRIDS, 3, CAP, 1))(owners_keys, owners_turns).reshape((COLS, WINDOWS, 3))
    live = place_ends((jax.random.randint(splits[4], (COLS, WINDOWS, 3), 0, 3) < 2).astype(jnp.int32), jax.random.fold_in(splits[4], 1), 0, 1)
    place = place_ends(jax.random.randint(splits[5], (COLS, WINDOWS, 3), 0, POS), jax.random.fold_in(splits[5], 1), 0, POS - 1).astype(jnp.int32)
    return dict(strip=strip, screen_first=screen_first, screen_second=screen_second, owners=owners, live=live, place=place)


def dft_table(length, direction):
    index = jnp.arange(length, dtype=jnp.int32)
    phase = index[:, None] * index[None, :] % length
    angle = phase.astype(jnp.float32) * (2.0 * math.pi / length)
    scale = 1.0 / math.sqrt(length)
    return (jnp.cos(angle) * scale, direction * jnp.sin(angle) * scale)

def left_apply(table, field):
    real_table, imag_table = table
    real_part, imag_part = field
    real = jnp.dot(real_table, real_part, preferred_element_type=jnp.float32) - jnp.dot(imag_table, imag_part, preferred_element_type=jnp.float32)
    imag = jnp.dot(real_table, imag_part, preferred_element_type=jnp.float32) + jnp.dot(imag_table, real_part, preferred_element_type=jnp.float32)
    return (real, imag)

def right_apply(field, table):
    real_table, imag_table = table
    real_part, imag_part = field
    real = jnp.dot(real_part, real_table, preferred_element_type=jnp.float32) - jnp.dot(imag_part, imag_table, preferred_element_type=jnp.float32)
    imag = jnp.dot(real_part, imag_table, preferred_element_type=jnp.float32) + jnp.dot(imag_part, real_table, preferred_element_type=jnp.float32)
    return (real, imag)

def screen_apply(field, screen):
    real_part, imag_part = field
    screen_real = screen[0].astype(jnp.float32)
    screen_imag = screen[1].astype(jnp.float32)
    real = real_part * screen_real - imag_part * screen_imag
    imag = real_part * screen_imag + imag_part * screen_real
    return (real.astype(jnp.bfloat16), imag.astype(jnp.bfloat16))

def process_tiles(tiles, screen_first, screen_second, forward, inverse):
    tile_count, width = tiles.shape
    side_tiles = math.isqrt(tile_count)
    win_size = math.isqrt(width // 2)
    sub_size = side_tiles * win_size
    field = tiles.reshape(side_tiles, side_tiles, 2, win_size, win_size).transpose(2, 0, 3, 1, 4).reshape(2, sub_size, sub_size)
    rows = left_apply(forward, (field[0], field[1]))
    rows = (rows[0].astype(jnp.bfloat16), rows[1].astype(jnp.bfloat16))
    spectrum = screen_apply(right_apply(rows, forward), screen_first)
    back = left_apply(inverse, spectrum)
    back = (back[0].astype(jnp.bfloat16), back[1].astype(jnp.bfloat16))
    image = screen_apply(right_apply(back, inverse), screen_second)
    stacked = jnp.stack([image[0], image[1]])
    return stacked.reshape(2, side_tiles, win_size, side_tiles, win_size).transpose(1, 3, 0, 2, 4).reshape(tile_count, width)

def reference(strip, screen_first, screen_second, owners, live, place):
    width = 2 * WIN * WIN
    small_real, small_imag = dft_table(WIN, -1.0)
    small = (small_real.astype(jnp.bfloat16), small_imag.astype(jnp.bfloat16))
    front = left_apply(small, (strip[0], strip[1]))
    contrib = jnp.stack([front[0], front[1]]).astype(jnp.bfloat16)
    windows = contrib.reshape(2, WIN, WINDOWS, WIN).transpose(2, 0, 1, 3).reshape(WINDOWS, width)
    big_real, big_imag = dft_table(SUB, -1.0)
    forward = (big_real.astype(jnp.bfloat16), big_imag.astype(jnp.bfloat16))
    inverse = (big_real.astype(jnp.bfloat16), (-big_imag).astype(jnp.bfloat16))
    widened = windows.astype(jnp.float32)
    summed = jnp.zeros((WINDOWS, width), jnp.float32)
    for column in range(N_COL):
        target = (owners[column] * POS + place[column]).astype(jnp.int32)
        weight = live[column].astype(jnp.float32)
        embedded = jnp.zeros((SUBGRIDS * POS, width), jnp.float32)
        for member in range(3):
            embedded = embedded + jax.ops.segment_sum(widened * weight[:, member, None], target[:, member], num_segments=SUBGRIDS * POS)
        tiles = embedded.astype(jnp.bfloat16).reshape(SUBGRIDS, POS, width)
        processed = lax.map(lambda block: process_tiles(block, screen_first, screen_second, forward, inverse), tiles)
        flat = processed.reshape(SUBGRIDS * POS, width)
        for member in range(3):
            summed = summed + flat[target[:, member]].astype(jnp.float32) * weight[:, member, None]
    field = summed.reshape(WINDOWS, 2, WIN, WIN).transpose(1, 2, 0, 3).reshape(2, WIN, WINDOWS * WIN)
    back_real, back_imag = dft_table(WIN, 1.0)
    highest = lax.Precision.HIGHEST
    real = jnp.dot(back_real, field[0], precision=highest) - jnp.dot(back_imag, field[1], precision=highest)
    imag = jnp.dot(back_real, field[1], precision=highest) + jnp.dot(back_imag, field[0], precision=highest)
    return jnp.stack([real, imag])
```

```python
import math

import functools

import jax
import jax.numpy as jnp
import numpy as np
from jax import lax
from jax.experimental import pallas as pl
from jax.experimental.pallas import tpu as pltpu
from jax.sharding import PartitionSpec as P

SUB_DEV = 2


def dft_table(length, direction):
    index = jnp.arange(length, dtype=jnp.int32)
    phase = index[:, None] * index[None, :] % length
    angle = phase.astype(jnp.float32) * (2.0 * math.pi / length)
    scale = 1.0 / math.sqrt(length)
    return (jnp.cos(angle) * scale, direction * jnp.sin(angle) * scale)


def left_apply(table, field):
    real_table, imag_table = table
    real_part, imag_part = field
    real = jnp.dot(real_table, real_part, preferred_element_type=jnp.float32) - jnp.dot(
        imag_table, imag_part, preferred_element_type=jnp.float32
    )
    imag = jnp.dot(real_table, imag_part, preferred_element_type=jnp.float32) + jnp.dot(
        imag_table, real_part, preferred_element_type=jnp.float32
    )
    return (real, imag)


def right_apply(field, table):
    real_table, imag_table = table
    real_part, imag_part = field
    real = jnp.dot(real_part, real_table, preferred_element_type=jnp.float32) - jnp.dot(
        imag_part, imag_table, preferred_element_type=jnp.float32
    )
    imag = jnp.dot(real_part, imag_table, preferred_element_type=jnp.float32) + jnp.dot(
        imag_part, real_table, preferred_element_type=jnp.float32
    )
    return (real, imag)


def screen_apply(field, screen):
    real_part, imag_part = field
    screen_real = screen[0].astype(jnp.float32)
    screen_imag = screen[1].astype(jnp.float32)
    real = real_part * screen_real - imag_part * screen_imag
    imag = real_part * screen_imag + imag_part * screen_real
    return (real.astype(jnp.bfloat16), imag.astype(jnp.bfloat16))


def process_tiles(tiles, screen_first, screen_second, forward, inverse):
    tile_count, width = tiles.shape
    side_tiles = math.isqrt(tile_count)
    win_size = math.isqrt(width // 2)
    sub_size = side_tiles * win_size
    field = (
        tiles.reshape(side_tiles, side_tiles, 2, win_size, win_size)
        .transpose(2, 0, 3, 1, 4)
        .reshape(2, sub_size, sub_size)
    )
    rows = left_apply(forward, (field[0], field[1]))
    rows = (rows[0].astype(jnp.bfloat16), rows[1].astype(jnp.bfloat16))
    spectrum = screen_apply(right_apply(rows, forward), screen_first)
    back = left_apply(inverse, spectrum)
    back = (back[0].astype(jnp.bfloat16), back[1].astype(jnp.bfloat16))
    image = screen_apply(right_apply(back, inverse), screen_second)
    stacked = jnp.stack([image[0], image[1]])
    return (
        stacked.reshape(2, side_tiles, win_size, side_tiles, win_size)
        .transpose(1, 3, 0, 2, 4)
        .reshape(tile_count, width)
    )


def exchanged(strip, screen_first, screen_second, owners, live, place):
    win_size = strip.shape[1]
    sub_size = screen_first.shape[-1]
    side_tiles = sub_size // win_size
    tile_count = side_tiles * side_tiles
    width = 2 * win_size * win_size
    peer_count = lax.axis_size("facet")
    win_local = strip.shape[2] // win_size
    sub_local = SUB_DEV
    subgrid_count = sub_local * peer_count
    capacity = max(2, (7 * win_local + 2 * subgrid_count - 1) // (2 * subgrid_count))
    total_slots = subgrid_count * capacity
    small_real, small_imag = dft_table(win_size, -1.0)
    small = (small_real.astype(jnp.bfloat16), small_imag.astype(jnp.bfloat16))
    front = left_apply(small, (strip[0], strip[1]))
    contrib = jnp.stack([front[0], front[1]]).astype(jnp.bfloat16)
    windows = (
        contrib.reshape(2, win_size, win_local, win_size)
        .transpose(2, 0, 1, 3)
        .reshape(win_local, width)
    )
    flat_owner = owners[0].reshape(-1)
    flat_live = live[0].reshape(-1)
    flat_place = place[0].reshape(-1)
    entries = flat_owner.shape[0]
    order_index = jnp.arange(entries, dtype=jnp.int32)
    earlier = (flat_owner[:, None] == flat_owner[None, :]) & (
        order_index[None, :] < order_index[:, None]
    )
    rank = jnp.sum(earlier.astype(jnp.int32), axis=1)
    slot_of = flat_owner * capacity + rank
    slot_index = jnp.arange(total_slots, dtype=jnp.int32)
    hit_rows = ((slot_of[None, :] == slot_index[:, None]) & (flat_live[None, :] == 1)).astype(
        jnp.int32
    )
    hit_cols = ((slot_of[:, None] == slot_index[None, :]) & (flat_live[:, None] == 1)).astype(
        jnp.int32
    )
    codes = jnp.sum(hit_rows * (flat_place[None, :] + 1), axis=1) - 1
    packer = jnp.sum(hit_rows.reshape(total_slots, win_local, 3), axis=2).astype(jnp.bfloat16)
    unpacker = jnp.sum(hit_cols.reshape(win_local, 3, total_slots), axis=1).astype(jnp.bfloat16)
    outgoing = jnp.dot(packer, windows, preferred_element_type=jnp.float32).astype(jnp.bfloat16)
    outgoing = outgoing.reshape(peer_count, sub_local, capacity, width)
    codes = codes.reshape(peer_count, sub_local, capacity)
    big_real, big_imag = dft_table(sub_size, -1.0)
    forward = (big_real.astype(jnp.bfloat16), big_imag.astype(jnp.bfloat16))
    inverse = (big_real.astype(jnp.bfloat16), (-big_imag).astype(jnp.bfloat16))
    tile_index = jnp.arange(tile_count, dtype=jnp.int32)
    parcels = lax.all_to_all(outgoing, "facet", split_axis=0, concat_axis=0, tiled=True)
    labels = lax.all_to_all(codes, "facet", split_axis=0, concat_axis=0, tiled=True)
    item_count = parcels.shape[1]
    sources = parcels.shape[0]
    stacked = parcels.transpose(1, 0, 2, 3).reshape(item_count, sources * capacity, width)
    marks = labels.transpose(1, 0, 2).reshape(item_count, sources * capacity)

    def one_subgrid(pair):
        slabs, tags = pair
        embed_map = (tags[None, :] == tile_index[:, None]).astype(jnp.bfloat16)
        cut_map = (tags[:, None] == tile_index[None, :]).astype(jnp.bfloat16)
        tiles = jnp.dot(embed_map, slabs, preferred_element_type=jnp.float32).astype(jnp.bfloat16)
        finished = process_tiles(tiles, screen_first, screen_second, forward, inverse)
        return jnp.dot(cut_map, finished, preferred_element_type=jnp.float32).astype(jnp.bfloat16)

    result = lax.map(one_subgrid, (stacked, marks))
    returned = lax.all_to_all(
        result.reshape(item_count, sources, capacity, width).transpose(1, 0, 2, 3),
        "facet",
        split_axis=0,
        concat_axis=0,
        tiled=True,
    )
    summed = jnp.dot(
        unpacker, returned.reshape(total_slots, width), preferred_element_type=jnp.float32
    )
    field = (
        summed.reshape(win_local, 2, win_size, win_size)
        .transpose(1, 2, 0, 3)
        .reshape(2, win_size, win_local * win_size)
    )
    column = lax.psum_scatter(
        field.astype(jnp.bfloat16), "col", scatter_dimension=2, tiled=True
    ).astype(jnp.float32)
    back_real, back_imag = dft_table(win_size, 1.0)
    highest = lax.Precision.HIGHEST
    real = jnp.dot(back_real, column[0], precision=highest) - jnp.dot(
        back_imag, column[1], precision=highest
    )
    imag = jnp.dot(back_real, column[1], precision=highest) + jnp.dot(
        back_imag, column[0], precision=highest
    )
    return jnp.stack([real, imag])


GATHER_BYTES = 16 << 20


def host_table(length):
    index = np.arange(length, dtype=np.int64)
    angle = (index[:, None] * index[None, :] % length) * (2.0 * math.pi / length)
    scale = 1.0 / math.sqrt(length)
    return np.cos(angle) * scale, -np.sin(angle) * scale


def rounded_pair(pair):
    return tuple(part.astype(jnp.bfloat16).astype(np.float64) for part in pair)


def left_block(real, imag):
    return np.concatenate(
        [np.concatenate([real, -imag], axis=1), np.concatenate([imag, real], axis=1)], axis=0
    )


def blocks_body(front_ref, big_ref, first_ref, forward_ref, inverse_ref):
    half = big_ref.shape[1]
    low, high = pl.ds(0, half), pl.ds(half, half)
    first_ref[low, low] = front_ref[0]
    first_ref[low, high] = -front_ref[1]
    first_ref[high, low] = front_ref[1]
    first_ref[high, high] = front_ref[0]
    forward_ref[low, low] = big_ref[0]
    forward_ref[low, high] = big_ref[1]
    forward_ref[high, low] = -big_ref[1]
    forward_ref[high, high] = big_ref[0]
    inverse_ref[low, low] = big_ref[0]
    inverse_ref[low, high] = -big_ref[1]
    inverse_ref[high, low] = big_ref[1]
    inverse_ref[high, high] = big_ref[0]


def table_blocks(sub_size, win_size):
    big = rounded_pair(host_table(sub_size))
    small = rounded_pair(host_table(win_size))
    eye = np.eye(sub_size // win_size)
    wide = (np.kron(eye, small[0]), np.kron(eye, small[1]))
    front = (big[0] @ wide[0] - big[1] @ wide[1], big[0] @ wide[1] + big[1] @ wide[0])
    front = np.stack(front).astype(jnp.bfloat16)
    stacked = np.stack(big).astype(jnp.bfloat16)
    full = jax.ShapeDtypeStruct((2 * sub_size, 2 * sub_size), jnp.bfloat16)
    vmem = pl.BlockSpec(memory_space=pltpu.VMEM)
    return pl.pallas_call(
        blocks_body, out_shape=[full] * 3, in_specs=[vmem] * 2, out_specs=[vmem] * 3, name="blocks"
    )(jnp.asarray(front), jnp.asarray(stacked))


def local_body(
    sub_local,
    codes_ref,
    strips_ref,
    screen_first_ref,
    screen_second_ref,
    first_ref,
    forward_ref,
    inverse_ref,
    out_ref,
    field,
    tall,
    flat,
):
    peers, _, capacity = codes_ref.shape
    win = strips_ref.shape[2]
    size = screen_first_ref.shape[1]
    tiles = size // win
    pair = 2 * win
    part_windows = out_ref.shape[3] // win
    parts = out_ref.shape[0] // peers
    base = lax.axis_index("facet") * sub_local
    lane_half = lax.broadcasted_iota(jnp.int32, (win, pair), 1) // win
    step = size // 2

    def zero_out(index, carry):
        out_ref[index] = jnp.zeros(out_ref.shape[1:], out_ref.dtype)
        return carry

    lax.fori_loop(0, out_ref.shape[0], zero_out, 0)

    def entries(subgrid, visit):
        def peer_loop(peer, carry):
            def slot_loop(slot, inner):
                code = codes_ref[peer, subgrid, slot]

                @pl.when(code >= 0)
                def _():
                    spot = code % (tiles * tiles)
                    visit(peer, code // (tiles * tiles), spot // tiles, spot % tiles)

                return inner

            return lax.fori_loop(0, capacity, slot_loop, carry)

        lax.fori_loop(0, peers, peer_loop, 0)

    def one_subgrid(number, carry):
        subgrid = base + number
        field[...] = jnp.zeros(field.shape, field.dtype)

        def embed(peer, window, row, column):
            lanes = pl.ds(pl.multiple_of(window // 2 * pair, pair), pair)
            target = pl.ds(pl.multiple_of(column // 2 * pair, pair), pair)
            shift = (window + column) % 2 * win
            for part in range(2):
                piece = strips_ref[peer, part, :, lanes].astype(jnp.float32)
                piece = pltpu.roll(piece, shift, 1)
                rows = pl.ds(pl.multiple_of(part * size + row * win, win), win)
                field[rows, target] += jnp.where(lane_half == column % 2, piece, 0.0)

        entries(subgrid, embed)
        tall[...] = field[...].astype(jnp.bfloat16)

        def left(table_ref):
            for part in range(2):
                for half in range(2):
                    rows = pl.ds(part * size + half * step, step)
                    flat[pl.ds(half * step, step), pl.ds(part * size, size)] = jnp.dot(
                        table_ref[rows, :], tall[...], preferred_element_type=jnp.float32
                    ).astype(jnp.bfloat16)

        def right(table_ref, screen_ref):
            for half in range(2):
                rows = pl.ds(half * step, step)
                product = jnp.dot(flat[rows, :], table_ref[...], preferred_element_type=jnp.float32)
                real_part, imag_part = product[:, :size], product[:, size:]
                screen_real = screen_ref[0, rows, :].astype(jnp.float32)
                screen_imag = screen_ref[1, rows, :].astype(jnp.float32)
                tall[rows, :] = (real_part * screen_real - imag_part * screen_imag).astype(
                    jnp.bfloat16
                )
                tall[pl.ds(size + half * step, step), :] = (
                    real_part * screen_imag + imag_part * screen_real
                ).astype(jnp.bfloat16)

        left(first_ref)
        right(forward_ref, screen_first_ref)
        left(forward_ref)
        right(inverse_ref, screen_second_ref)

        def cut(peer, window, row, column):
            source = pl.ds(pl.multiple_of(column // 2 * pair, pair), pair)
            spot = window % part_windows
            lanes = pl.ds(pl.multiple_of(spot // 2 * pair, pair), pair)
            slab = peer * parts + window // part_windows
            shift = (window + column) % 2 * win
            for part in range(2):
                rows = pl.ds(pl.multiple_of(part * size + row * win, win), win)
                piece = pltpu.roll(tall[rows, source].astype(jnp.float32), shift, 1)
                held = out_ref[slab, part, :, lanes].astype(jnp.float32)
                out_ref[slab, part, :, lanes] = (
                    held + jnp.where(lane_half == window % 2, piece, 0.0)
                ).astype(out_ref.dtype)

        entries(subgrid, cut)
        return carry

    lax.fori_loop(0, sub_local, one_subgrid, 0)


def entry_codes(owners, live, place, subgrid_count, tile_count):
    win_local = owners.shape[1]
    capacity = max(2, (7 * win_local + 2 * subgrid_count - 1) // (2 * subgrid_count))
    owner = owners[0].reshape(-1)
    count = owner.shape[0]
    window = jnp.arange(count, dtype=jnp.int32) // 3
    label = window * tile_count + place[0].reshape(-1) + 1
    order = jnp.arange(count, dtype=jnp.int32)
    earlier = (owner[:, None] == owner[None, :]) & (order[None, :] < order[:, None])
    rank = jnp.sum(earlier.astype(jnp.int32), axis=1)
    slot = jnp.where(live[0].reshape(-1) == 1, owner * capacity + rank, -1)
    slots = jnp.arange(subgrid_count * capacity, dtype=jnp.int32)
    hit = slot[None, :] == slots[:, None]
    codes = jnp.sum(jnp.where(hit, label[None, :], 0), axis=1) - 1
    return codes.reshape(subgrid_count, capacity)


def gathered(strip, screen_first, screen_second, owners, live, place):
    win_size = strip.shape[1]
    sub_size = screen_first.shape[-1]
    tile_count = (sub_size // win_size) ** 2
    peer_count = lax.axis_size("facet")
    parts = lax.axis_size("col")
    sub_local = SUB_DEV
    codes = entry_codes(owners, live, place, sub_local * peer_count, tile_count)
    codes = lax.all_gather(codes, "facet")
    strips = lax.all_gather(strip, "facet")
    first, forward, inverse = table_blocks(sub_size, win_size)
    piece = strip.shape[2] // parts
    vmem = pl.BlockSpec(memory_space=pltpu.VMEM)
    partial = pl.pallas_call(
        functools.partial(local_body, sub_local),
        out_shape=jax.ShapeDtypeStruct((peer_count * parts, 2, win_size, piece), jnp.bfloat16),
        in_specs=[pl.BlockSpec(memory_space=pltpu.SMEM)] + [vmem] * 6,
        out_specs=vmem,
        scratch_shapes=[
            pltpu.VMEM((2 * sub_size, sub_size), jnp.float32),
            pltpu.VMEM((2 * sub_size, sub_size), jnp.bfloat16),
            pltpu.VMEM((sub_size, 2 * sub_size), jnp.bfloat16),
        ],
        compiler_params=pltpu.CompilerParams(vmem_limit_bytes=56 << 20),
        name="local",
    )(codes, strips, screen_first, screen_second, first, forward, inverse)
    mine = lax.psum_scatter(partial, ("facet", "col"), scatter_dimension=0, tiled=True)
    return finish(mine.reshape(2 * win_size, piece), win_size)


def finish(mine, win_size):
    real, imag = host_table(win_size)
    table = jnp.asarray(left_block(real, -imag).astype(np.float32))
    image = jnp.dot(table, mine.astype(jnp.float32), precision=lax.Precision.HIGHEST)
    return image.reshape(2, win_size, mine.shape[1])


def shards(strip, screen_first, screen_second, owners, live, place):
    if strip.size * strip.dtype.itemsize * lax.axis_size("facet") <= GATHER_BYTES:
        return gathered(strip, screen_first, screen_second, owners, live, place)
    return exchanged(strip, screen_first, screen_second, owners, live, place)


def solution(mesh):
    placed = (
        P(None, None, "facet"),
        P(),
        P(),
        P("col", "facet", None),
        P("col", "facet", None),
        P("col", "facet", None),
    )
    return jax.shard_map(
        shards,
        mesh=mesh,
        in_specs=placed,
        out_specs=P(None, None, ("facet", "col")),
        check_vma=False,
    )
```

```python
import math

import functools

import jax
import jax.numpy as jnp
import numpy as np
from jax import lax
from jax.experimental import pallas as pl
from jax.experimental.pallas import tpu as pltpu
from jax.sharding import PartitionSpec as P

SUB_DEV = 2


def dft_table(length, direction):
    index = jnp.arange(length, dtype=jnp.int32)
    phase = index[:, None] * index[None, :] % length
    angle = phase.astype(jnp.float32) * (2.0 * math.pi / length)
    scale = 1.0 / math.sqrt(length)
    return (jnp.cos(angle) * scale, direction * jnp.sin(angle) * scale)


def left_apply(table, field):
    real_table, imag_table = table
    real_part, imag_part = field
    real = jnp.dot(real_table, real_part, preferred_element_type=jnp.float32) - jnp.dot(
        imag_table, imag_part, preferred_element_type=jnp.float32
    )
    imag = jnp.dot(real_table, imag_part, preferred_element_type=jnp.float32) + jnp.dot(
        imag_table, real_part, preferred_element_type=jnp.float32
    )
    return (real, imag)


def right_apply(field, table):
    real_table, imag_table = table
    real_part, imag_part = field
    real = jnp.dot(real_part, real_table, preferred_element_type=jnp.float32) - jnp.dot(
        imag_part, imag_table, preferred_element_type=jnp.float32
    )
    imag = jnp.dot(real_part, imag_table, preferred_element_type=jnp.float32) + jnp.dot(
        imag_part, real_table, preferred_element_type=jnp.float32
    )
    return (real, imag)


def screen_apply(field, screen):
    real_part, imag_part = field
    screen_real = screen[0].astype(jnp.float32)
    screen_imag = screen[1].astype(jnp.float32)
    real = real_part * screen_real - imag_part * screen_imag
    imag = real_part * screen_imag + imag_part * screen_real
    return (real.astype(jnp.bfloat16), imag.astype(jnp.bfloat16))


def process_tiles(tiles, screen_first, screen_second, forward, inverse):
    tile_count, width = tiles.shape
    side_tiles = math.isqrt(tile_count)
    win_size = math.isqrt(width // 2)
    sub_size = side_tiles * win_size
    field = (
        tiles.reshape(side_tiles, side_tiles, 2, win_size, win_size)
        .transpose(2, 0, 3, 1, 4)
        .reshape(2, sub_size, sub_size)
    )
    rows = left_apply(forward, (field[0], field[1]))
    rows = (rows[0].astype(jnp.bfloat16), rows[1].astype(jnp.bfloat16))
    spectrum = screen_apply(right_apply(rows, forward), screen_first)
    back = left_apply(inverse, spectrum)
    back = (back[0].astype(jnp.bfloat16), back[1].astype(jnp.bfloat16))
    image = screen_apply(right_apply(back, inverse), screen_second)
    stacked = jnp.stack([image[0], image[1]])
    return (
        stacked.reshape(2, side_tiles, win_size, side_tiles, win_size)
        .transpose(1, 3, 0, 2, 4)
        .reshape(tile_count, width)
    )


def exchanged(strip, screen_first, screen_second, owners, live, place):
    win_size = strip.shape[1]
    sub_size = screen_first.shape[-1]
    side_tiles = sub_size // win_size
    tile_count = side_tiles * side_tiles
    width = 2 * win_size * win_size
    peer_count = lax.axis_size("facet")
    win_local = strip.shape[2] // win_size
    sub_local = SUB_DEV
    subgrid_count = sub_local * peer_count
    capacity = max(2, (7 * win_local + 2 * subgrid_count - 1) // (2 * subgrid_count))
    total_slots = subgrid_count * capacity
    small_real, small_imag = dft_table(win_size, -1.0)
    small = (small_real.astype(jnp.bfloat16), small_imag.astype(jnp.bfloat16))
    front = left_apply(small, (strip[0], strip[1]))
    contrib = jnp.stack([front[0], front[1]]).astype(jnp.bfloat16)
    windows = (
        contrib.reshape(2, win_size, win_local, win_size)
        .transpose(2, 0, 1, 3)
        .reshape(win_local, width)
    )
    flat_owner = owners[0].reshape(-1)
    flat_live = live[0].reshape(-1)
    flat_place = place[0].reshape(-1)
    entries = flat_owner.shape[0]
    order_index = jnp.arange(entries, dtype=jnp.int32)
    earlier = (flat_owner[:, None] == flat_owner[None, :]) & (
        order_index[None, :] < order_index[:, None]
    )
    rank = jnp.sum(earlier.astype(jnp.int32), axis=1)
    slot_of = flat_owner * capacity + rank
    slot_index = jnp.arange(total_slots, dtype=jnp.int32)
    hit_rows = ((slot_of[None, :] == slot_index[:, None]) & (flat_live[None, :] == 1)).astype(
        jnp.int32
    )
    hit_cols = ((slot_of[:, None] == slot_index[None, :]) & (flat_live[:, None] == 1)).astype(
        jnp.int32
    )
    codes = jnp.sum(hit_rows * (flat_place[None, :] + 1), axis=1) - 1
    packer = jnp.sum(hit_rows.reshape(total_slots, win_local, 3), axis=2).astype(jnp.bfloat16)
    unpacker = jnp.sum(hit_cols.reshape(win_local, 3, total_slots), axis=1).astype(jnp.bfloat16)
    outgoing = jnp.dot(packer, windows, preferred_element_type=jnp.float32).astype(jnp.bfloat16)
    outgoing = outgoing.reshape(peer_count, sub_local, capacity, width)
    codes = codes.reshape(peer_count, sub_local, capacity)
    big_real, big_imag = dft_table(sub_size, -1.0)
    forward = (big_real.astype(jnp.bfloat16), big_imag.astype(jnp.bfloat16))
    inverse = (big_real.astype(jnp.bfloat16), (-big_imag).astype(jnp.bfloat16))
    tile_index = jnp.arange(tile_count, dtype=jnp.int32)
    parcels = lax.all_to_all(outgoing, "facet", split_axis=0, concat_axis=0, tiled=True)
    labels = lax.all_to_all(codes, "facet", split_axis=0, concat_axis=0, tiled=True)
    item_count = parcels.shape[1]
    sources = parcels.shape[0]
    stacked = parcels.transpose(1, 0, 2, 3).reshape(item_count, sources * capacity, width)
    marks = labels.transpose(1, 0, 2).reshape(item_count, sources * capacity)

    def one_subgrid(pair):
        slabs, tags = pair
        embed_map = (tags[None, :] == tile_index[:, None]).astype(jnp.bfloat16)
        cut_map = (tags[:, None] == tile_index[None, :]).astype(jnp.bfloat16)
        tiles = jnp.dot(embed_map, slabs, preferred_element_type=jnp.float32).astype(jnp.bfloat16)
        finished = process_tiles(tiles, screen_first, screen_second, forward, inverse)
        return jnp.dot(cut_map, finished, preferred_element_type=jnp.float32).astype(jnp.bfloat16)

    result = lax.map(one_subgrid, (stacked, marks))
    returned = lax.all_to_all(
        result.reshape(item_count, sources, capacity, width).transpose(1, 0, 2, 3),
        "facet",
        split_axis=0,
        concat_axis=0,
        tiled=True,
    )
    summed = jnp.dot(
        unpacker, returned.reshape(total_slots, width), preferred_element_type=jnp.float32
    )
    field = (
        summed.reshape(win_local, 2, win_size, win_size)
        .transpose(1, 2, 0, 3)
        .reshape(2, win_size, win_local * win_size)
    )
    column = lax.psum_scatter(
        field.astype(jnp.bfloat16), "col", scatter_dimension=2, tiled=True
    ).astype(jnp.float32)
    back_real, back_imag = dft_table(win_size, 1.0)
    highest = lax.Precision.HIGHEST
    real = jnp.dot(back_real, column[0], precision=highest) - jnp.dot(
        back_imag, column[1], precision=highest
    )
    imag = jnp.dot(back_real, column[1], precision=highest) + jnp.dot(
        back_imag, column[0], precision=highest
    )
    return jnp.stack([real, imag])


GATHER_BYTES = 16 << 20


def host_table(length):
    index = np.arange(length, dtype=np.int64)
    angle = (index[:, None] * index[None, :] % length) * (2.0 * math.pi / length)
    scale = 1.0 / math.sqrt(length)
    return np.cos(angle) * scale, -np.sin(angle) * scale


def rounded_pair(pair):
    return tuple(part.astype(jnp.bfloat16).astype(np.float64) for part in pair)


def left_block(real, imag):
    return np.concatenate(
        [np.concatenate([real, -imag], axis=1), np.concatenate([imag, real], axis=1)], axis=0
    )


def fill_blocks(front_ref, big_ref, first_ref, forward_ref, inverse_ref):
    half = big_ref.shape[1]
    low, high = pl.ds(0, half), pl.ds(half, half)
    first_ref[low, low] = front_ref[0]
    first_ref[low, high] = -front_ref[1]
    first_ref[high, low] = front_ref[1]
    first_ref[high, high] = front_ref[0]
    forward_ref[low, low] = big_ref[0]
    forward_ref[low, high] = big_ref[1]
    forward_ref[high, low] = -big_ref[1]
    forward_ref[high, high] = big_ref[0]
    inverse_ref[low, low] = big_ref[0]
    inverse_ref[low, high] = -big_ref[1]
    inverse_ref[high, low] = big_ref[1]
    inverse_ref[high, high] = big_ref[0]


def table_pairs(sub_size, win_size):
    big = rounded_pair(host_table(sub_size))
    small = rounded_pair(host_table(win_size))
    eye = np.eye(sub_size // win_size)
    wide = (np.kron(eye, small[0]), np.kron(eye, small[1]))
    front = (big[0] @ wide[0] - big[1] @ wide[1], big[0] @ wide[1] + big[1] @ wide[0])
    return np.stack(front).astype(jnp.bfloat16), np.stack(big).astype(jnp.bfloat16)


def meet(partners):
    barrier = pltpu.get_barrier_semaphore()
    for partner in partners:
        pl.semaphore_signal(
            barrier, inc=1, device_id=partner, device_id_type=pl.DeviceIdType.MESH
        )
    pl.semaphore_wait(barrier, len(partners))


def gather_body(
    peers,
    strip_ref,
    codes_ref,
    front_ref,
    big_ref,
    out_ref,
    all_codes_ref,
    first_out,
    forward_out,
    inverse_out,
    first_ref,
    forward_ref,
    inverse_ref,
    send_sem,
    recv_sem,
    code_send,
    code_recv,
    local_sem,
):
    levels = peers // 2
    facet, col = lax.axis_index("facet"), lax.axis_index("col")
    z, y = facet // 2, facet % 2
    x, core = col // 2, col % 2
    half = strip_ref.shape[1] // 2
    higher = [lax.rem(z + d, levels) for d in range(1, levels)]
    z_peers = [(level * 2 + y, col) for level in higher]
    y_peer = (z * 2 + 1 - y, col)
    x_peer = (facet, (1 - x) * 2 + core)
    core_peer = (facet, x * 2 + 1 - core)
    corners = [(level * 2 + 1 - y, col) for level in higher]
    meet(z_peers + [y_peer, x_peer, core_peer] + corners)
    started = []

    def piece(ref, x_at, core_at):
        return ref.at[x_at, pl.ds(pl.multiple_of(core_at * half, half), half)]

    def send(source, item, x_at, core_at, kind, target):
        copy = pltpu.make_async_remote_copy(
            src_ref=piece(source, x_at, core_at),
            dst_ref=piece(out_ref.at[item], x_at, core_at),
            send_sem=send_sem.at[len(started)],
            recv_sem=recv_sem.at[kind, item],
            device_id=target,
            device_id_type=pl.DeviceIdType.MESH,
        )
        copy.start()
        started.append(copy)

    def arrived(item, x_at, core_at, kind):
        pltpu.make_async_copy(
            piece(out_ref.at[item], x_at, core_at),
            piece(out_ref.at[item], x_at, core_at),
            recv_sem.at[kind, item],
        ).wait()

    send(strip_ref, facet, x, core, 0, y_peer)
    for target in z_peers:
        send(strip_ref, facet, x, core, 0, target)
    codes_sent = []
    for number, target in enumerate([y_peer] + z_peers + corners):
        copy = pltpu.make_async_remote_copy(
            src_ref=codes_ref,
            dst_ref=all_codes_ref.at[facet],
            send_sem=code_send.at[number],
            recv_sem=code_recv.at[facet],
            device_id=target,
            device_id_type=pl.DeviceIdType.MESH,
        )
        copy.start()
        codes_sent.append(copy)
    kept = [
        pltpu.make_async_copy(strip_ref, out_ref.at[facet], local_sem.at[0]),
        pltpu.make_async_copy(codes_ref, all_codes_ref.at[facet], local_sem.at[1]),
    ]
    for copy in kept:
        copy.start()
    fill_blocks(front_ref, big_ref, first_ref, forward_ref, inverse_ref)
    for number, (source, target) in enumerate(
        [(first_ref, first_out), (forward_ref, forward_out), (inverse_ref, inverse_out)]
    ):
        copy = pltpu.make_async_copy(source, target, local_sem.at[2 + number])
        copy.start()
        kept.append(copy)

    def pass_on(item, kind, x_at):
        arrived(item, x_at, core, kind)
        send(out_ref.at[item], item, x_at, core, kind + 2, core_peer)

    order = [z] + higher
    for number, level in enumerate(order):
        same, other = level * 2 + y, level * 2 + 1 - y
        if number > 0:
            arrived(same, x, core, 0)
            send(out_ref.at[same], same, x, core, 0, y_peer)
            send(out_ref.at[same], same, x, core, 1, x_peer)
            send(out_ref.at[same], same, x, core, 2, core_peer)
        arrived(other, x, core, 0)
        send(out_ref.at[other], other, x, core, 1, x_peer)
        send(out_ref.at[other], other, x, core, 2, core_peer)
    for number, level in enumerate(order):
        if number > 0:
            pass_on(level * 2 + y, 1, 1 - x)
        pass_on(level * 2 + 1 - y, 1, 1 - x)
    for number, level in enumerate(order):
        for item in [level * 2 + y, level * 2 + 1 - y][number == 0 :]:
            arrived(item, x, 1 - core, 2)
            arrived(item, 1 - x, 1 - core, 3)
            pltpu.make_async_copy(
                all_codes_ref.at[item], all_codes_ref.at[item], code_recv.at[item]
            ).wait()
    for copy in started + codes_sent:
        copy.wait_send()
    for copy in kept:
        copy.wait()


def gather_strips(strip, codes, peers, sub_size, win_size):
    front, big = table_pairs(sub_size, win_size)
    full = (2 * sub_size, 2 * sub_size)
    lanes = 128
    padded = jnp.pad(codes, ((0, 0), (0, lanes - codes.shape[1])), constant_values=-1)
    vmem = pl.BlockSpec(memory_space=pltpu.VMEM)
    anywhere = pl.BlockSpec(memory_space=pl.ANY)
    levels = peers // 2
    copies = levels + 3 * (levels - 1) + 2 * levels + 2 * levels - 1
    return pl.pallas_call(
        functools.partial(gather_body, peers),
        out_shape=[
            jax.ShapeDtypeStruct((peers,) + strip.shape, strip.dtype),
            jax.ShapeDtypeStruct((peers,) + padded.shape, padded.dtype),
        ]
        + [jax.ShapeDtypeStruct(full, jnp.bfloat16)] * 3,
        in_specs=[vmem] * 4,
        out_specs=[anywhere] * 5,
        scratch_shapes=[pltpu.VMEM(full, jnp.bfloat16)] * 3
        + [
            pltpu.SemaphoreType.DMA((copies,)),
            pltpu.SemaphoreType.DMA((4, peers)),
            pltpu.SemaphoreType.DMA((peers,)),
            pltpu.SemaphoreType.DMA((peers,)),
            pltpu.SemaphoreType.DMA((5,)),
        ],
        compiler_params=pltpu.CompilerParams(collective_id=0, has_side_effects=True),
        name="gather",
    )(strip, padded, jnp.asarray(front), jnp.asarray(big))


def reduce_body(
    levels,
    partial_ref,
    out_ref,
    held,
    from_core,
    from_x_wide,
    from_y_wide,
    from_y,
    from_x,
    done,
    from_z,
    send_sem,
    recv_sem,
    z_send,
    z_recv,
    local_sem,
):
    facet, col = lax.axis_index("facet"), lax.axis_index("col")
    z, y = facet // 2, facet % 2
    x, core = col // 2, col % 2
    half = out_ref.shape[1] // 2
    top, bottom = pl.ds(0, half), pl.ds(half, half)
    order = [lax.rem(z + d, levels) for d in range(1, levels)] + [z]
    z_peers = [(level * 2 + y, col) for level in order[:-1]]
    y_peer = (z * 2 + 1 - y, col)
    x_peer = (facet, (1 - x) * 2 + core)
    core_peer = (facet, x * 2 + 1 - core)
    meet(z_peers + [y_peer, x_peer, core_peer])
    sent = []

    def send(source, target, kind, number, peer):
        copy = pltpu.make_async_remote_copy(
            src_ref=source,
            dst_ref=target,
            send_sem=send_sem.at[kind, number],
            recv_sem=recv_sem.at[kind, number],
            device_id=peer,
            device_id_type=pl.DeviceIdType.MESH,
        )
        copy.start()
        sent.append(copy)
        return copy

    def add(target, left, right):
        target[...] = (left[...].astype(jnp.float32) + right[...].astype(jnp.float32)).astype(
            target.dtype
        )

    first, kept = [], []
    for number, level in enumerate(order):
        first.append(
            send(partial_ref.at[1 - core, level], from_core.at[number], 0, number, core_peer)
        )
        copy = pltpu.make_async_copy(
            partial_ref.at[core, level], held.at[number], local_sem.at[number]
        )
        copy.start()
        kept.append(copy)
    wide_x, wide_y, narrow_x, narrow_y, across = [], [], [], [], []

    def join_cores(number):
        kept[number].wait()
        first[number].wait_recv()

        def body(index, carry):
            y_at, x_at, part = index // 4, index // 2 % 2, index % 2
            add(
                held.at[number, y_at, x_at, part],
                held.at[number, y_at, x_at, part],
                from_core.at[number, y_at, x_at, part],
            )
            return carry

        lax.fori_loop(0, 8, body, 0)
        wide_x.append(
            send(held.at[number, :, 1 - x, :, top], from_x_wide.at[number], 1, number, x_peer)
        )
        wide_y.append(
            send(held.at[number, 1 - y, :, :, bottom], from_y_wide.at[number], 2, number, y_peer)
        )

    def join_wide(number):
        wide_x[number].wait_recv()

        def body_x(index, carry):
            place = held.at[number, index // 2, x, index % 2, top]
            add(place, place, from_x_wide.at[number, index // 2, index % 2])
            return carry

        lax.fori_loop(0, 4, body_x, 0)
        narrow_y.append(
            send(held.at[number, 1 - y, x, :, top], from_y.at[number], 3, number, y_peer)
        )
        wide_y[number].wait_recv()

        def body_y(index, carry):
            place = held.at[number, y, index // 2, index % 2, bottom]
            add(place, place, from_y_wide.at[number, index // 2, index % 2])
            return carry

        lax.fori_loop(0, 4, body_y, 0)
        narrow_x.append(
            send(held.at[number, y, 1 - x, :, bottom], from_x.at[number], 4, number, x_peer)
        )

    def join_narrow(number):
        narrow_y[number].wait_recv()
        for part in range(2):
            add(
                done.at[number, part, top],
                held.at[number, y, x, part, top],
                from_y.at[number, part],
            )
        narrow_x[number].wait_recv()
        for part in range(2):
            add(
                done.at[number, part, bottom],
                held.at[number, y, x, part, bottom],
                from_x.at[number, part],
            )
        if number < levels - 1:
            copy = pltpu.make_async_remote_copy(
                src_ref=done.at[number],
                dst_ref=from_z.at[number],
                send_sem=z_send.at[number],
                recv_sem=z_recv.at[number],
                device_id=z_peers[number],
                device_id_type=pl.DeviceIdType.MESH,
            )
            copy.start()
            across.append(copy)

    for step in range(levels + 2):
        if step < levels:
            join_cores(step)
        if 0 <= step - 1 < levels:
            join_wide(step - 1)
        if 0 <= step - 2 < levels:
            join_narrow(step - 2)
    for copy in across:
        copy.wait_recv()
    for part in range(2):
        total = done[levels - 1, part].astype(jnp.float32)
        for number in range(levels - 1):
            total += from_z[number, part].astype(jnp.float32)
        out_ref[part] = total
    for copy in sent + across:
        copy.wait_send()


def reduce_partials(partial, levels, win_size, width):
    kind = partial.dtype
    half = win_size // 2
    return pl.pallas_call(
        functools.partial(reduce_body, levels),
        out_shape=jax.ShapeDtypeStruct((2, win_size, width), jnp.float32),
        in_specs=[pl.BlockSpec(memory_space=pl.ANY)],
        out_specs=pl.BlockSpec(memory_space=pltpu.VMEM),
        scratch_shapes=[
            pltpu.VMEM((levels, 2, 2, 2, win_size, width), kind),
            pltpu.VMEM((levels, 2, 2, 2, win_size, width), kind),
            pltpu.VMEM((levels, 2, 2, half, width), kind),
            pltpu.VMEM((levels, 2, 2, half, width), kind),
            pltpu.VMEM((levels, 2, half, width), kind),
            pltpu.VMEM((levels, 2, half, width), kind),
            pltpu.VMEM((levels, 2, win_size, width), kind),
            pltpu.VMEM((levels - 1, 2, win_size, width), kind),
            pltpu.SemaphoreType.DMA((5, levels)),
            pltpu.SemaphoreType.DMA((5, levels)),
            pltpu.SemaphoreType.DMA((levels - 1,)),
            pltpu.SemaphoreType.DMA((levels - 1,)),
            pltpu.SemaphoreType.DMA((levels,)),
        ],
        compiler_params=pltpu.CompilerParams(
            collective_id=1, has_side_effects=True, vmem_limit_bytes=40 << 20
        ),
        name="reduce",
    )(partial.reshape(2, levels, 2, 2, 2, win_size, width))


def local_body(
    sub_local,
    capacity,
    codes_ref,
    strips_ref,
    screen_first_ref,
    screen_second_ref,
    first_ref,
    forward_ref,
    inverse_ref,
    out_ref,
    field,
    tall,
    flat,
):
    peers = codes_ref.shape[0]
    win = strips_ref.shape[2]
    size = screen_first_ref.shape[1]
    tiles = size // win
    pair = 2 * win
    part_windows = out_ref.shape[3] // win
    parts = out_ref.shape[0] // peers
    base = lax.axis_index("facet") * sub_local
    lane_half = lax.broadcasted_iota(jnp.int32, (win, pair), 1) // win
    step = size // 2

    def zero_out(index, carry):
        out_ref[index] = jnp.zeros(out_ref.shape[1:], out_ref.dtype)
        return carry

    lax.fori_loop(0, out_ref.shape[0], zero_out, 0)

    def entries(subgrid, visit):
        def peer_loop(peer, carry):
            def slot_loop(slot, inner):
                code = codes_ref[peer, subgrid, slot]

                @pl.when(code >= 0)
                def _():
                    spot = code % (tiles * tiles)
                    visit(peer, code // (tiles * tiles), spot // tiles, spot % tiles)

                return inner

            return lax.fori_loop(0, capacity, slot_loop, carry)

        lax.fori_loop(0, peers, peer_loop, 0)

    def one_subgrid(number, carry):
        subgrid = base + number
        field[...] = jnp.zeros(field.shape, field.dtype)

        def embed(peer, window, row, column):
            lanes = pl.ds(pl.multiple_of(window // 2 * pair, pair), pair)
            target = pl.ds(pl.multiple_of(column // 2 * pair, pair), pair)
            shift = (window + column) % 2 * win
            for part in range(2):
                piece = strips_ref[peer, part, :, lanes].astype(jnp.float32)
                piece = pltpu.roll(piece, shift, 1)
                rows = pl.ds(pl.multiple_of(part * size + row * win, win), win)
                field[rows, target] += jnp.where(lane_half == column % 2, piece, 0.0)

        entries(subgrid, embed)
        tall[...] = field[...].astype(jnp.bfloat16)

        def left(table_ref):
            for part in range(2):
                for half in range(2):
                    rows = pl.ds(part * size + half * step, step)
                    flat[pl.ds(half * step, step), pl.ds(part * size, size)] = jnp.dot(
                        table_ref[rows, :], tall[...], preferred_element_type=jnp.float32
                    ).astype(jnp.bfloat16)

        def right(table_ref, screen_ref):
            for half in range(2):
                rows = pl.ds(half * step, step)
                product = jnp.dot(flat[rows, :], table_ref[...], preferred_element_type=jnp.float32)
                real_part, imag_part = product[:, :size], product[:, size:]
                screen_real = screen_ref[0, rows, :].astype(jnp.float32)
                screen_imag = screen_ref[1, rows, :].astype(jnp.float32)
                tall[rows, :] = (real_part * screen_real - imag_part * screen_imag).astype(
                    jnp.bfloat16
                )
                tall[pl.ds(size + half * step, step), :] = (
                    real_part * screen_imag + imag_part * screen_real
                ).astype(jnp.bfloat16)

        left(first_ref)
        right(forward_ref, screen_first_ref)
        left(forward_ref)
        right(inverse_ref, screen_second_ref)

        def cut(peer, window, row, column):
            source = pl.ds(pl.multiple_of(column // 2 * pair, pair), pair)
            spot = window % part_windows
            lanes = pl.ds(pl.multiple_of(spot // 2 * pair, pair), pair)
            part_index = window // part_windows
            slab = (part_index % 2 * peers + peer) * (parts // 2) + part_index // 2
            shift = (window + column) % 2 * win
            for part in range(2):
                rows = pl.ds(pl.multiple_of(part * size + row * win, win), win)
                piece = pltpu.roll(tall[rows, source].astype(jnp.float32), shift, 1)
                held = out_ref[slab, part, :, lanes].astype(jnp.float32)
                out_ref[slab, part, :, lanes] = (
                    held + jnp.where(lane_half == window % 2, piece, 0.0)
                ).astype(out_ref.dtype)

        entries(subgrid, cut)
        return carry

    lax.fori_loop(0, sub_local, one_subgrid, 0)


def entry_codes(owners, live, place, subgrid_count, tile_count):
    win_local = owners.shape[1]
    capacity = max(2, (7 * win_local + 2 * subgrid_count - 1) // (2 * subgrid_count))
    owner = owners[0].reshape(-1)
    count = owner.shape[0]
    window = jnp.arange(count, dtype=jnp.int32) // 3
    label = window * tile_count + place[0].reshape(-1) + 1
    order = jnp.arange(count, dtype=jnp.int32)
    earlier = (owner[:, None] == owner[None, :]) & (order[None, :] < order[:, None])
    rank = jnp.sum(earlier.astype(jnp.int32), axis=1)
    slot = jnp.where(live[0].reshape(-1) == 1, owner * capacity + rank, -1)
    slots = jnp.arange(subgrid_count * capacity, dtype=jnp.int32)
    hit = slot[None, :] == slots[:, None]
    codes = jnp.sum(jnp.where(hit, label[None, :], 0), axis=1) - 1
    return codes.reshape(subgrid_count, capacity)


def gathered(strip, screen_first, screen_second, owners, live, place):
    win_size = strip.shape[1]
    sub_size = screen_first.shape[-1]
    tile_count = (sub_size // win_size) ** 2
    peer_count = lax.axis_size("facet")
    parts = lax.axis_size("col")
    sub_local = SUB_DEV
    codes = entry_codes(owners, live, place, sub_local * peer_count, tile_count)
    capacity = codes.shape[1]
    strips, codes, first, forward, inverse = gather_strips(
        strip, codes, peer_count, sub_size, win_size
    )
    piece = strip.shape[2] // parts
    vmem = pl.BlockSpec(memory_space=pltpu.VMEM)
    partial = pl.pallas_call(
        functools.partial(local_body, sub_local, capacity),
        out_shape=jax.ShapeDtypeStruct((peer_count * parts, 2, win_size, piece), jnp.bfloat16),
        in_specs=[pl.BlockSpec(memory_space=pltpu.SMEM)] + [vmem] * 6,
        out_specs=vmem,
        scratch_shapes=[
            pltpu.VMEM((2 * sub_size, sub_size), jnp.float32),
            pltpu.VMEM((2 * sub_size, sub_size), jnp.bfloat16),
            pltpu.VMEM((sub_size, 2 * sub_size), jnp.bfloat16),
        ],
        compiler_params=pltpu.CompilerParams(vmem_limit_bytes=56 << 20),
        name="local",
    )(codes, strips, screen_first, screen_second, first, forward, inverse)
    mine = reduce_partials(partial, peer_count // 2, win_size, piece)
    return finish(mine.reshape(2 * win_size, piece), win_size)


def finish(mine, win_size):
    real, imag = host_table(win_size)
    table = jnp.asarray(left_block(real, -imag).astype(np.float32))
    image = jnp.dot(table, mine, precision=lax.Precision.HIGHEST)
    return image.reshape(2, win_size, mine.shape[1])


def shards(strip, screen_first, screen_second, owners, live, place):
    paired = lax.axis_size("facet") % 2 == 0 and lax.axis_size("col") == 4
    if paired and strip.size * strip.dtype.itemsize * lax.axis_size("facet") <= GATHER_BYTES:
        return gathered(strip, screen_first, screen_second, owners, live, place)
    return exchanged(strip, screen_first, screen_second, owners, live, place)


def solution(mesh):
    placed = (
        P(None, None, "facet"),
        P(),
        P(),
        P("col", "facet", None),
        P("col", "facet", None),
        P("col", "facet", None),
    )
    return jax.shard_map(
        shards,
        mesh=mesh,
        in_specs=placed,
        out_specs=P(None, None, ("facet", "col")),
        check_vma=False,
    )
```

```python
import math

import functools

import jax
import jax.numpy as jnp
import numpy as np
from jax import lax
from jax.experimental import pallas as pl
from jax.experimental.pallas import tpu as pltpu
from jax.sharding import PartitionSpec as P

SUB_DEV = 2


def dft_table(length, direction):
    index = jnp.arange(length, dtype=jnp.int32)
    phase = index[:, None] * index[None, :] % length
    angle = phase.astype(jnp.float32) * (2.0 * math.pi / length)
    scale = 1.0 / math.sqrt(length)
    return (jnp.cos(angle) * scale, direction * jnp.sin(angle) * scale)


def left_apply(table, field):
    real_table, imag_table = table
    real_part, imag_part = field
    real = jnp.dot(real_table, real_part, preferred_element_type=jnp.float32) - jnp.dot(
        imag_table, imag_part, preferred_element_type=jnp.float32
    )
    imag = jnp.dot(real_table, imag_part, preferred_element_type=jnp.float32) + jnp.dot(
        imag_table, real_part, preferred_element_type=jnp.float32
    )
    return (real, imag)


def right_apply(field, table):
    real_table, imag_table = table
    real_part, imag_part = field
    real = jnp.dot(real_part, real_table, preferred_element_type=jnp.float32) - jnp.dot(
        imag_part, imag_table, preferred_element_type=jnp.float32
    )
    imag = jnp.dot(real_part, imag_table, preferred_element_type=jnp.float32) + jnp.dot(
        imag_part, real_table, preferred_element_type=jnp.float32
    )
    return (real, imag)


def screen_apply(field, screen):
    real_part, imag_part = field
    screen_real = screen[0].astype(jnp.float32)
    screen_imag = screen[1].astype(jnp.float32)
    real = real_part * screen_real - imag_part * screen_imag
    imag = real_part * screen_imag + imag_part * screen_real
    return (real.astype(jnp.bfloat16), imag.astype(jnp.bfloat16))


def process_tiles(tiles, screen_first, screen_second, forward, inverse):
    tile_count, width = tiles.shape
    side_tiles = math.isqrt(tile_count)
    win_size = math.isqrt(width // 2)
    sub_size = side_tiles * win_size
    field = (
        tiles.reshape(side_tiles, side_tiles, 2, win_size, win_size)
        .transpose(2, 0, 3, 1, 4)
        .reshape(2, sub_size, sub_size)
    )
    rows = left_apply(forward, (field[0], field[1]))
    rows = (rows[0].astype(jnp.bfloat16), rows[1].astype(jnp.bfloat16))
    spectrum = screen_apply(right_apply(rows, forward), screen_first)
    back = left_apply(inverse, spectrum)
    back = (back[0].astype(jnp.bfloat16), back[1].astype(jnp.bfloat16))
    image = screen_apply(right_apply(back, inverse), screen_second)
    stacked = jnp.stack([image[0], image[1]])
    return (
        stacked.reshape(2, side_tiles, win_size, side_tiles, win_size)
        .transpose(1, 3, 0, 2, 4)
        .reshape(tile_count, width)
    )


def exchanged(strip, screen_first, screen_second, owners, live, place):
    win_size = strip.shape[1]
    sub_size = screen_first.shape[-1]
    side_tiles = sub_size // win_size
    tile_count = side_tiles * side_tiles
    width = 2 * win_size * win_size
    peer_count = lax.axis_size("facet")
    win_local = strip.shape[2] // win_size
    sub_local = SUB_DEV
    subgrid_count = sub_local * peer_count
    capacity = max(2, (7 * win_local + 2 * subgrid_count - 1) // (2 * subgrid_count))
    total_slots = subgrid_count * capacity
    small_real, small_imag = dft_table(win_size, -1.0)
    small = (small_real.astype(jnp.bfloat16), small_imag.astype(jnp.bfloat16))
    front = left_apply(small, (strip[0], strip[1]))
    contrib = jnp.stack([front[0], front[1]]).astype(jnp.bfloat16)
    windows = (
        contrib.reshape(2, win_size, win_local, win_size)
        .transpose(2, 0, 1, 3)
        .reshape(win_local, width)
    )
    flat_owner = owners[0].reshape(-1)
    flat_live = live[0].reshape(-1)
    flat_place = place[0].reshape(-1)
    entries = flat_owner.shape[0]
    order_index = jnp.arange(entries, dtype=jnp.int32)
    earlier = (flat_owner[:, None] == flat_owner[None, :]) & (
        order_index[None, :] < order_index[:, None]
    )
    rank = jnp.sum(earlier.astype(jnp.int32), axis=1)
    slot_of = flat_owner * capacity + rank
    slot_index = jnp.arange(total_slots, dtype=jnp.int32)
    hit_rows = ((slot_of[None, :] == slot_index[:, None]) & (flat_live[None, :] == 1)).astype(
        jnp.int32
    )
    hit_cols = ((slot_of[:, None] == slot_index[None, :]) & (flat_live[:, None] == 1)).astype(
        jnp.int32
    )
    codes = jnp.sum(hit_rows * (flat_place[None, :] + 1), axis=1) - 1
    packer = jnp.sum(hit_rows.reshape(total_slots, win_local, 3), axis=2).astype(jnp.bfloat16)
    unpacker = jnp.sum(hit_cols.reshape(win_local, 3, total_slots), axis=1).astype(jnp.bfloat16)
    outgoing = jnp.dot(packer, windows, preferred_element_type=jnp.float32).astype(jnp.bfloat16)
    outgoing = outgoing.reshape(peer_count, sub_local, capacity, width)
    codes = codes.reshape(peer_count, sub_local, capacity)
    big_real, big_imag = dft_table(sub_size, -1.0)
    forward = (big_real.astype(jnp.bfloat16), big_imag.astype(jnp.bfloat16))
    inverse = (big_real.astype(jnp.bfloat16), (-big_imag).astype(jnp.bfloat16))
    tile_index = jnp.arange(tile_count, dtype=jnp.int32)
    parcels = lax.all_to_all(outgoing, "facet", split_axis=0, concat_axis=0, tiled=True)
    labels = lax.all_to_all(codes, "facet", split_axis=0, concat_axis=0, tiled=True)
    item_count = parcels.shape[1]
    sources = parcels.shape[0]
    stacked = parcels.transpose(1, 0, 2, 3).reshape(item_count, sources * capacity, width)
    marks = labels.transpose(1, 0, 2).reshape(item_count, sources * capacity)

    def one_subgrid(pair):
        slabs, tags = pair
        embed_map = (tags[None, :] == tile_index[:, None]).astype(jnp.bfloat16)
        cut_map = (tags[:, None] == tile_index[None, :]).astype(jnp.bfloat16)
        tiles = jnp.dot(embed_map, slabs, preferred_element_type=jnp.float32).astype(jnp.bfloat16)
        finished = process_tiles(tiles, screen_first, screen_second, forward, inverse)
        return jnp.dot(cut_map, finished, preferred_element_type=jnp.float32).astype(jnp.bfloat16)

    result = lax.map(one_subgrid, (stacked, marks))
    returned = lax.all_to_all(
        result.reshape(item_count, sources, capacity, width).transpose(1, 0, 2, 3),
        "facet",
        split_axis=0,
        concat_axis=0,
        tiled=True,
    )
    summed = jnp.dot(
        unpacker, returned.reshape(total_slots, width), preferred_element_type=jnp.float32
    )
    field = (
        summed.reshape(win_local, 2, win_size, win_size)
        .transpose(1, 2, 0, 3)
        .reshape(2, win_size, win_local * win_size)
    )
    column = lax.psum_scatter(
        field.astype(jnp.bfloat16), "col", scatter_dimension=2, tiled=True
    ).astype(jnp.float32)
    back_real, back_imag = dft_table(win_size, 1.0)
    highest = lax.Precision.HIGHEST
    real = jnp.dot(back_real, column[0], precision=highest) - jnp.dot(
        back_imag, column[1], precision=highest
    )
    imag = jnp.dot(back_real, column[1], precision=highest) + jnp.dot(
        back_imag, column[0], precision=highest
    )
    return jnp.stack([real, imag])


GATHER_BYTES = 16 << 20
UNROLL = 4


def host_table(length):
    index = np.arange(length, dtype=np.int64)
    angle = (index[:, None] * index[None, :] % length) * (2.0 * math.pi / length)
    scale = 1.0 / math.sqrt(length)
    return np.cos(angle) * scale, -np.sin(angle) * scale


def rounded_pair(pair):
    return tuple(part.astype(jnp.bfloat16).astype(np.float64) for part in pair)


def left_block(real, imag):
    return np.concatenate(
        [np.concatenate([real, -imag], axis=1), np.concatenate([imag, real], axis=1)], axis=0
    )


def fill_blocks(front_ref, big_ref, first_ref, forward_ref, inverse_ref):
    half = big_ref.shape[1]
    low, high = pl.ds(0, half), pl.ds(half, half)
    first_ref[low, low] = front_ref[0]
    first_ref[low, high] = -front_ref[1]
    first_ref[high, low] = front_ref[1]
    first_ref[high, high] = front_ref[0]
    forward_ref[low, low] = big_ref[0]
    forward_ref[low, high] = big_ref[1]
    forward_ref[high, low] = -big_ref[1]
    forward_ref[high, high] = big_ref[0]
    inverse_ref[low, low] = big_ref[0]
    inverse_ref[low, high] = -big_ref[1]
    inverse_ref[high, low] = big_ref[1]
    inverse_ref[high, high] = big_ref[0]


def table_pairs(sub_size, win_size):
    big = rounded_pair(host_table(sub_size))
    small = rounded_pair(host_table(win_size))
    eye = np.eye(sub_size // win_size)
    wide = (np.kron(eye, small[0]), np.kron(eye, small[1]))
    front = (big[0] @ wide[0] - big[1] @ wide[1], big[0] @ wide[1] + big[1] @ wide[0])
    return np.stack(front).astype(jnp.bfloat16), np.stack(big).astype(jnp.bfloat16)


def meet(partners):
    barrier = pltpu.get_barrier_semaphore()
    for partner in partners:
        pl.semaphore_signal(
            barrier, inc=1, device_id=partner, device_id_type=pl.DeviceIdType.MESH
        )
    pl.semaphore_wait(barrier, len(partners))


def gather_body(
    peers,
    strip_ref,
    codes_ref,
    front_ref,
    big_ref,
    out_ref,
    all_codes_ref,
    first_out,
    forward_out,
    inverse_out,
    first_ref,
    forward_ref,
    inverse_ref,
    send_sem,
    recv_sem,
    code_send,
    code_recv,
    local_sem,
):
    levels = peers // 2
    facet, col = lax.axis_index("facet"), lax.axis_index("col")
    z, y = facet // 2, facet % 2
    x, core = col // 2, col % 2
    half = strip_ref.shape[1] // 2
    higher = [lax.rem(z + d, levels) for d in range(1, levels)]
    z_peers = [(level * 2 + y, col) for level in higher]
    y_peer = (z * 2 + 1 - y, col)
    x_peer = (facet, (1 - x) * 2 + core)
    core_peer = (facet, x * 2 + 1 - core)
    corners = [(level * 2 + 1 - y, col) for level in higher]
    meet(z_peers + [y_peer, x_peer, core_peer] + corners)
    started = []

    def piece(ref, x_at, core_at):
        return ref.at[x_at, pl.ds(pl.multiple_of(core_at * half, half), half)]

    def send(source, item, x_at, core_at, kind, target):
        copy = pltpu.make_async_remote_copy(
            src_ref=piece(source, x_at, core_at),
            dst_ref=piece(out_ref.at[item], x_at, core_at),
            send_sem=send_sem.at[len(started)],
            recv_sem=recv_sem.at[kind, item],
            device_id=target,
            device_id_type=pl.DeviceIdType.MESH,
        )
        copy.start()
        started.append(copy)

    def arrived(item, x_at, core_at, kind):
        pltpu.make_async_copy(
            piece(out_ref.at[item], x_at, core_at),
            piece(out_ref.at[item], x_at, core_at),
            recv_sem.at[kind, item],
        ).wait()

    send(strip_ref, facet, x, core, 0, y_peer)
    for target in z_peers:
        send(strip_ref, facet, x, core, 0, target)
    codes_sent = []
    for number, target in enumerate([y_peer] + z_peers + corners):
        copy = pltpu.make_async_remote_copy(
            src_ref=codes_ref,
            dst_ref=all_codes_ref.at[facet],
            send_sem=code_send.at[number],
            recv_sem=code_recv.at[facet],
            device_id=target,
            device_id_type=pl.DeviceIdType.MESH,
        )
        copy.start()
        codes_sent.append(copy)
    kept = [
        pltpu.make_async_copy(strip_ref, out_ref.at[facet], local_sem.at[0]),
        pltpu.make_async_copy(codes_ref, all_codes_ref.at[facet], local_sem.at[1]),
    ]
    for copy in kept:
        copy.start()
    fill_blocks(front_ref, big_ref, first_ref, forward_ref, inverse_ref)
    for number, (source, target) in enumerate(
        [(first_ref, first_out), (forward_ref, forward_out), (inverse_ref, inverse_out)]
    ):
        copy = pltpu.make_async_copy(source, target, local_sem.at[2 + number])
        copy.start()
        kept.append(copy)

    def pass_on(item, kind, x_at):
        arrived(item, x_at, core, kind)
        send(out_ref.at[item], item, x_at, core, kind + 2, core_peer)

    order = [z] + higher
    for number, level in enumerate(order):
        same, other = level * 2 + y, level * 2 + 1 - y
        if number > 0:
            arrived(same, x, core, 0)
            send(out_ref.at[same], same, x, core, 0, y_peer)
            send(out_ref.at[same], same, x, core, 1, x_peer)
            send(out_ref.at[same], same, x, core, 2, core_peer)
        arrived(other, x, core, 0)
        send(out_ref.at[other], other, x, core, 1, x_peer)
        send(out_ref.at[other], other, x, core, 2, core_peer)
    for number, level in enumerate(order):
        if number > 0:
            pass_on(level * 2 + y, 1, 1 - x)
        pass_on(level * 2 + 1 - y, 1, 1 - x)
    for number, level in enumerate(order):
        for item in [level * 2 + y, level * 2 + 1 - y][number == 0 :]:
            arrived(item, x, 1 - core, 2)
            arrived(item, 1 - x, 1 - core, 3)
            pltpu.make_async_copy(
                all_codes_ref.at[item], all_codes_ref.at[item], code_recv.at[item]
            ).wait()
    for copy in started + codes_sent:
        copy.wait_send()
    for copy in kept:
        copy.wait()


def gather_strips(strip, codes, peers, sub_size, win_size):
    front, big = table_pairs(sub_size, win_size)
    full = (2 * sub_size, 2 * sub_size)
    lanes = 128
    padded = jnp.pad(codes, ((0, 0), (0, lanes - codes.shape[1])), constant_values=-1)
    vmem = pl.BlockSpec(memory_space=pltpu.VMEM)
    anywhere = pl.BlockSpec(memory_space=pl.ANY)
    levels = peers // 2
    copies = levels + 3 * (levels - 1) + 2 * levels + 2 * levels - 1
    return pl.pallas_call(
        functools.partial(gather_body, peers),
        out_shape=[
            jax.ShapeDtypeStruct((peers,) + strip.shape, strip.dtype),
            jax.ShapeDtypeStruct((peers,) + padded.shape, padded.dtype),
        ]
        + [jax.ShapeDtypeStruct(full, jnp.bfloat16)] * 3,
        in_specs=[vmem] * 4,
        out_specs=[anywhere] * 5,
        scratch_shapes=[pltpu.VMEM(full, jnp.bfloat16)] * 3
        + [
            pltpu.SemaphoreType.DMA((copies,)),
            pltpu.SemaphoreType.DMA((4, peers)),
            pltpu.SemaphoreType.DMA((peers,)),
            pltpu.SemaphoreType.DMA((peers,)),
            pltpu.SemaphoreType.DMA((5,)),
        ],
        compiler_params=pltpu.CompilerParams(collective_id=0, has_side_effects=True),
        name="gather",
    )(strip, padded, jnp.asarray(front), jnp.asarray(big))


def reduce_body(
    levels,
    partial_ref,
    out_ref,
    held,
    from_core,
    from_x_wide,
    from_y_wide,
    from_y,
    from_x,
    done,
    from_z,
    send_sem,
    recv_sem,
    z_send,
    z_recv,
    local_sem,
):
    facet, col = lax.axis_index("facet"), lax.axis_index("col")
    z, y = facet // 2, facet % 2
    x, core = col // 2, col % 2
    half = out_ref.shape[1] // 2
    top, bottom = pl.ds(0, half), pl.ds(half, half)
    order = [lax.rem(z + d, levels) for d in range(1, levels)] + [z]
    z_peers = [(level * 2 + y, col) for level in order[:-1]]
    y_peer = (z * 2 + 1 - y, col)
    x_peer = (facet, (1 - x) * 2 + core)
    core_peer = (facet, x * 2 + 1 - core)
    meet(z_peers + [y_peer, x_peer, core_peer])
    sent = []

    def send(source, target, kind, number, peer):
        copy = pltpu.make_async_remote_copy(
            src_ref=source,
            dst_ref=target,
            send_sem=send_sem.at[kind, number],
            recv_sem=recv_sem.at[kind, number],
            device_id=peer,
            device_id_type=pl.DeviceIdType.MESH,
        )
        copy.start()
        sent.append(copy)
        return copy

    def add(target, left, right):
        target[...] = (left[...].astype(jnp.float32) + right[...].astype(jnp.float32)).astype(
            target.dtype
        )

    first, kept = [], []
    for number, level in enumerate(order):
        first.append(
            send(partial_ref.at[1 - core, level], from_core.at[number], 0, number, core_peer)
        )
        copy = pltpu.make_async_copy(
            partial_ref.at[core, level], held.at[number], local_sem.at[number]
        )
        copy.start()
        kept.append(copy)
    wide_x, wide_y, narrow_x, narrow_y, across = [], [], [], [], []

    def join_cores(number):
        kept[number].wait()
        first[number].wait_recv()

        def body(index, carry):
            y_at, x_at, part = index // 4, index // 2 % 2, index % 2
            add(
                held.at[number, y_at, x_at, part],
                held.at[number, y_at, x_at, part],
                from_core.at[number, y_at, x_at, part],
            )
            return carry

        lax.fori_loop(0, 8, body, 0)
        wide_x.append(
            send(held.at[number, :, 1 - x, :, top], from_x_wide.at[number], 1, number, x_peer)
        )
        wide_y.append(
            send(held.at[number, 1 - y, :, :, bottom], from_y_wide.at[number], 2, number, y_peer)
        )

    def join_wide(number):
        wide_x[number].wait_recv()

        def body_x(index, carry):
            place = held.at[number, index // 2, x, index % 2, top]
            add(place, place, from_x_wide.at[number, index // 2, index % 2])
            return carry

        lax.fori_loop(0, 4, body_x, 0)
        narrow_y.append(
            send(held.at[number, 1 - y, x, :, top], from_y.at[number], 3, number, y_peer)
        )
        wide_y[number].wait_recv()

        def body_y(index, carry):
            place = held.at[number, y, index // 2, index % 2, bottom]
            add(place, place, from_y_wide.at[number, index // 2, index % 2])
            return carry

        lax.fori_loop(0, 4, body_y, 0)
        narrow_x.append(
            send(held.at[number, y, 1 - x, :, bottom], from_x.at[number], 4, number, x_peer)
        )

    def join_narrow(number):
        narrow_y[number].wait_recv()
        for part in range(2):
            add(
                done.at[number, part, top],
                held.at[number, y, x, part, top],
                from_y.at[number, part],
            )
        narrow_x[number].wait_recv()
        for part in range(2):
            add(
                done.at[number, part, bottom],
                held.at[number, y, x, part, bottom],
                from_x.at[number, part],
            )
        if number < levels - 1:
            copy = pltpu.make_async_remote_copy(
                src_ref=done.at[number],
                dst_ref=from_z.at[number],
                send_sem=z_send.at[number],
                recv_sem=z_recv.at[number],
                device_id=z_peers[number],
                device_id_type=pl.DeviceIdType.MESH,
            )
            copy.start()
            across.append(copy)

    for step in range(levels + 2):
        if step < levels:
            join_cores(step)
        if 0 <= step - 1 < levels:
            join_wide(step - 1)
        if 0 <= step - 2 < levels:
            join_narrow(step - 2)
    for copy in across:
        copy.wait_recv()
    for part in range(2):
        total = done[levels - 1, part].astype(jnp.float32)
        for number in range(levels - 1):
            total += from_z[number, part].astype(jnp.float32)
        out_ref[part] = total
    for copy in sent + across:
        copy.wait_send()


def reduce_partials(partial, levels, win_size, width):
    kind = partial.dtype
    half = win_size // 2
    return pl.pallas_call(
        functools.partial(reduce_body, levels),
        out_shape=jax.ShapeDtypeStruct((2, win_size, width), jnp.float32),
        in_specs=[pl.BlockSpec(memory_space=pl.ANY)],
        out_specs=pl.BlockSpec(memory_space=pltpu.VMEM),
        scratch_shapes=[
            pltpu.VMEM((levels, 2, 2, 2, win_size, width), kind),
            pltpu.VMEM((levels, 2, 2, 2, win_size, width), kind),
            pltpu.VMEM((levels, 2, 2, half, width), kind),
            pltpu.VMEM((levels, 2, 2, half, width), kind),
            pltpu.VMEM((levels, 2, half, width), kind),
            pltpu.VMEM((levels, 2, half, width), kind),
            pltpu.VMEM((levels, 2, win_size, width), kind),
            pltpu.VMEM((levels - 1, 2, win_size, width), kind),
            pltpu.SemaphoreType.DMA((5, levels)),
            pltpu.SemaphoreType.DMA((5, levels)),
            pltpu.SemaphoreType.DMA((levels - 1,)),
            pltpu.SemaphoreType.DMA((levels - 1,)),
            pltpu.SemaphoreType.DMA((levels,)),
        ],
        compiler_params=pltpu.CompilerParams(
            collective_id=1, has_side_effects=True, vmem_limit_bytes=60 << 20
        ),
        name="reduce",
    )(partial.reshape(2, levels, 2, 2, 2, win_size, width))


def parted(value, count):
    if count & (count - 1) == 0:
        return lax.shift_right_logical(value, count.bit_length() - 1), value & (count - 1)
    return lax.div(value, count), lax.rem(value, count)


def local_body(
    sub_local,
    capacity,
    codes_ref,
    strips_hbm,
    screen_first_hbm,
    screen_second_hbm,
    first_hbm,
    forward_hbm,
    inverse_hbm,
    out_hbm,
    strips_ref,
    screen_first_ref,
    screen_second_ref,
    first_ref,
    forward_ref,
    inverse_ref,
    out_ref,
    field,
    tall_all,
    flat,
    listed,
    strip_sem,
    table_sem,
    out_sem,
):
    peers = codes_ref.shape[0]
    win = strips_ref.shape[2]
    win_local = strips_ref.shape[3] // win
    size = screen_first_ref.shape[1]
    tiles = size // win
    pair = 2 * win
    part_windows = out_ref.shape[3] // win
    parts = out_ref.shape[0] // peers
    base = lax.axis_index("facet") * sub_local
    lane_half = lax.broadcasted_iota(jnp.int32, (win, pair), 1) // win
    step = size // 2
    loads = [
        pltpu.make_async_copy(strips_hbm.at[peer], strips_ref.at[peer], strip_sem.at[peer])
        for peer in range(peers)
    ]
    tables = [
        pltpu.make_async_copy(source, target, table_sem.at[number])
        for number, (source, target) in enumerate(
            [
                (first_hbm, first_ref),
                (forward_hbm, forward_ref),
                (screen_first_hbm, screen_first_ref),
                (inverse_hbm, inverse_ref),
                (screen_second_hbm, screen_second_ref),
            ]
        )
    ]
    for copy in loads + tables:
        copy.start()

    def zero_out(index, carry):
        out_ref[index] = jnp.zeros(out_ref.shape[1:], out_ref.dtype)
        return carry

    lax.fori_loop(0, out_ref.shape[0], zero_out, 0)

    def list_up(number):
        def peer_loop(peer, count):
            for slot in range(capacity):
                code = codes_ref[peer, base + number, slot]
                listed[number, count] = peer * (win_local * tiles * tiles) + code
                count += (code >= 0).astype(jnp.int32)
            return count

        count = lax.fori_loop(0, peers, peer_loop, 0)
        for extra in range(UNROLL):
            listed[number, count + extra] = -1
        return lax.div(count + UNROLL - 1, UNROLL)

    rounds = [list_up(number) for number in range(sub_local)]

    def entry(number, index):
        value = listed[number, index]
        code = jnp.maximum(value, 0)
        peer, rest = parted(code, win_local * tiles * tiles)
        window, spot = parted(rest, tiles * tiles)
        row, column = parted(spot, tiles)
        return value >= 0, peer, window, row, column

    def embed_all(number):
        field[...] = jnp.zeros(field.shape, field.dtype)

        def body(turn, carry):
            todo = []
            for extra in range(UNROLL):
                valid, peer, window, row, column = entry(number, turn * UNROLL + extra)
                at, odd = parted(window, 2)
                lanes = pl.ds(pl.multiple_of(at * pair, pair), pair)
                at, column_odd = parted(column, 2)
                target = pl.ds(pl.multiple_of(at * pair, pair), pair)
                chosen = lane_half == jnp.where(valid, column_odd, 2)
                shift = (odd ^ column_odd) * win
                for part in range(2):
                    piece = strips_ref[peer, part, :, lanes].astype(jnp.float32)
                    piece = jnp.where(chosen, pltpu.roll(piece, shift, 1), 0.0)
                    rows = pl.ds(pl.multiple_of(part * size + row * win, win), win)
                    todo.append((rows, target, piece))
            for rows, target, piece in todo:
                field[rows, target] += piece
            return carry

        lax.fori_loop(0, rounds[number], body, 0)
        tall_all[number] = field[...].astype(jnp.bfloat16)

    for copy in loads:
        copy.wait()
    for number in range(sub_local):
        embed_all(number)
    for copy in tables:
        copy.wait()

    def transform(number, carry):
        tall = tall_all.at[number]

        def left(table_ref):
            for part in range(2):
                for half in range(2):
                    rows = pl.ds(part * size + half * step, step)
                    flat[pl.ds(half * step, step), pl.ds(part * size, size)] = jnp.dot(
                        table_ref[rows, :], tall[...], preferred_element_type=jnp.float32
                    ).astype(jnp.bfloat16)

        def right(table_ref, screen_ref):
            for half in range(2):
                rows = pl.ds(half * step, step)
                product = jnp.dot(flat[rows, :], table_ref[...], preferred_element_type=jnp.float32)
                real_part, imag_part = product[:, :size], product[:, size:]
                screen_real = screen_ref[0, rows, :].astype(jnp.float32)
                screen_imag = screen_ref[1, rows, :].astype(jnp.float32)
                tall[rows, :] = (real_part * screen_real - imag_part * screen_imag).astype(
                    jnp.bfloat16
                )
                tall[pl.ds(size + half * step, step), :] = (
                    real_part * screen_imag + imag_part * screen_real
                ).astype(jnp.bfloat16)

        left(first_ref)
        right(forward_ref, screen_first_ref)
        left(forward_ref)
        right(inverse_ref, screen_second_ref)
        return carry

    lax.fori_loop(0, sub_local, transform, 0)

    def cut_all(number):
        def body(turn, carry):
            todo = []
            for extra in range(UNROLL):
                valid, peer, window, row, column = entry(number, turn * UNROLL + extra)
                at, column_odd = parted(column, 2)
                source = pl.ds(pl.multiple_of(at * pair, pair), pair)
                part_index, spot = parted(window, part_windows)
                at, odd = parted(spot, 2)
                lanes = pl.ds(pl.multiple_of(at * pair, pair), pair)
                outer, inner = parted(part_index, 2)
                slab = (inner * peers + peer) * (parts // 2) + outer
                chosen = lane_half == jnp.where(valid, odd, 2)
                shift = (odd ^ column_odd) * win
                for part in range(2):
                    rows = pl.ds(pl.multiple_of(part * size + row * win, win), win)
                    piece = tall_all[number, rows, source].astype(jnp.float32)
                    piece = jnp.where(chosen, pltpu.roll(piece, shift, 1), 0.0)
                    todo.append((slab, part, lanes, piece))
            for slab, part, lanes, piece in todo:
                held = out_ref[slab, part, :, lanes].astype(jnp.float32)
                out_ref[slab, part, :, lanes] = (held + piece).astype(out_ref.dtype)
            return carry

        lax.fori_loop(0, rounds[number], body, 0)

    for number in range(sub_local):
        cut_all(number)
    copy = pltpu.make_async_copy(out_ref, out_hbm, out_sem)
    copy.start()
    copy.wait()


def entry_codes(owners, live, place, subgrid_count, tile_count):
    win_local = owners.shape[1]
    capacity = max(2, (7 * win_local + 2 * subgrid_count - 1) // (2 * subgrid_count))
    owner = owners[0].reshape(-1)
    count = owner.shape[0]
    window = jnp.arange(count, dtype=jnp.int32) // 3
    label = window * tile_count + place[0].reshape(-1) + 1
    order = jnp.arange(count, dtype=jnp.int32)
    earlier = (owner[:, None] == owner[None, :]) & (order[None, :] < order[:, None])
    rank = jnp.sum(earlier.astype(jnp.int32), axis=1)
    slot = jnp.where(live[0].reshape(-1) == 1, owner * capacity + rank, -1)
    slots = jnp.arange(subgrid_count * capacity, dtype=jnp.int32)
    hit = slot[None, :] == slots[:, None]
    codes = jnp.sum(jnp.where(hit, label[None, :], 0), axis=1) - 1
    return codes.reshape(subgrid_count, capacity)


def gathered(strip, screen_first, screen_second, owners, live, place):
    win_size = strip.shape[1]
    sub_size = screen_first.shape[-1]
    tile_count = (sub_size // win_size) ** 2
    peer_count = lax.axis_size("facet")
    parts = lax.axis_size("col")
    sub_local = SUB_DEV
    codes = entry_codes(owners, live, place, sub_local * peer_count, tile_count)
    capacity = codes.shape[1]
    strips, codes, first, forward, inverse = gather_strips(
        strip, codes, peer_count, sub_size, win_size
    )
    piece = strip.shape[2] // parts
    anywhere = pl.BlockSpec(memory_space=pl.ANY)
    slabs = (peer_count * parts, 2, win_size, piece)
    listing = -(-(peer_count * capacity + UNROLL) // 128) * 128
    partial = pl.pallas_call(
        functools.partial(local_body, sub_local, capacity),
        out_shape=jax.ShapeDtypeStruct(slabs, jnp.bfloat16),
        in_specs=[pl.BlockSpec(memory_space=pltpu.SMEM)] + [anywhere] * 6,
        out_specs=anywhere,
        scratch_shapes=[
            pltpu.VMEM(array.shape, array.dtype)
            for array in (strips, screen_first, screen_second, first, forward, inverse)
        ]
        + [
            pltpu.VMEM(slabs, jnp.bfloat16),
            pltpu.VMEM((2 * sub_size, sub_size), jnp.float32),
            pltpu.VMEM((sub_local, 2 * sub_size, sub_size), jnp.bfloat16),
            pltpu.VMEM((sub_size, 2 * sub_size), jnp.bfloat16),
            pltpu.SMEM((sub_local, listing), jnp.int32),
            pltpu.SemaphoreType.DMA((peer_count,)),
            pltpu.SemaphoreType.DMA((5,)),
            pltpu.SemaphoreType.DMA,
        ],
        compiler_params=pltpu.CompilerParams(vmem_limit_bytes=60 << 20),
        name="local",
    )(codes, strips, screen_first, screen_second, first, forward, inverse)
    mine = reduce_partials(partial, peer_count // 2, win_size, piece)
    return finish(mine.reshape(2 * win_size, piece), win_size)


def finish(mine, win_size):
    real, imag = host_table(win_size)
    table = jnp.asarray(left_block(real, -imag).astype(np.float32))
    image = jnp.dot(table, mine, precision=lax.Precision.HIGHEST)
    return image.reshape(2, win_size, mine.shape[1])


def shards(strip, screen_first, screen_second, owners, live, place):
    paired = lax.axis_size("facet") % 2 == 0 and lax.axis_size("col") == 4
    if paired and strip.size * strip.dtype.itemsize * lax.axis_size("facet") <= GATHER_BYTES:
        return gathered(strip, screen_first, screen_second, owners, live, place)
    return exchanged(strip, screen_first, screen_second, owners, live, place)


def solution(mesh):
    placed = (
        P(None, None, "facet"),
        P(),
        P(),
        P("col", "facet", None),
        P("col", "facet", None),
        P("col", "facet", None),
    )
    return jax.shard_map(
        shards,
        mesh=mesh,
        in_specs=placed,
        out_specs=P(None, None, ("facet", "col")),
        check_vma=False,
    )
```

```python
import math

import functools

import jax
import jax.numpy as jnp
import numpy as np
from jax import lax
from jax.experimental import pallas as pl
from jax.experimental.pallas import tpu as pltpu
from jax.sharding import PartitionSpec as P

SUB_DEV = 2


def dft_table(length, direction):
    index = jnp.arange(length, dtype=jnp.int32)
    phase = index[:, None] * index[None, :] % length
    angle = phase.astype(jnp.float32) * (2.0 * math.pi / length)
    scale = 1.0 / math.sqrt(length)
    return (jnp.cos(angle) * scale, direction * jnp.sin(angle) * scale)


def left_apply(table, field):
    real_table, imag_table = table
    real_part, imag_part = field
    real = jnp.dot(real_table, real_part, preferred_element_type=jnp.float32) - jnp.dot(
        imag_table, imag_part, preferred_element_type=jnp.float32
    )
    imag = jnp.dot(real_table, imag_part, preferred_element_type=jnp.float32) + jnp.dot(
        imag_table, real_part, preferred_element_type=jnp.float32
    )
    return (real, imag)


def right_apply(field, table):
    real_table, imag_table = table
    real_part, imag_part = field
    real = jnp.dot(real_part, real_table, preferred_element_type=jnp.float32) - jnp.dot(
        imag_part, imag_table, preferred_element_type=jnp.float32
    )
    imag = jnp.dot(real_part, imag_table, preferred_element_type=jnp.float32) + jnp.dot(
        imag_part, real_table, preferred_element_type=jnp.float32
    )
    return (real, imag)


def screen_apply(field, screen):
    real_part, imag_part = field
    screen_real = screen[0].astype(jnp.float32)
    screen_imag = screen[1].astype(jnp.float32)
    real = real_part * screen_real - imag_part * screen_imag
    imag = real_part * screen_imag + imag_part * screen_real
    return (real.astype(jnp.bfloat16), imag.astype(jnp.bfloat16))


def process_tiles(tiles, screen_first, screen_second, forward, inverse):
    tile_count, width = tiles.shape
    side_tiles = math.isqrt(tile_count)
    win_size = math.isqrt(width // 2)
    sub_size = side_tiles * win_size
    field = (
        tiles.reshape(side_tiles, side_tiles, 2, win_size, win_size)
        .transpose(2, 0, 3, 1, 4)
        .reshape(2, sub_size, sub_size)
    )
    rows = left_apply(forward, (field[0], field[1]))
    rows = (rows[0].astype(jnp.bfloat16), rows[1].astype(jnp.bfloat16))
    spectrum = screen_apply(right_apply(rows, forward), screen_first)
    back = left_apply(inverse, spectrum)
    back = (back[0].astype(jnp.bfloat16), back[1].astype(jnp.bfloat16))
    image = screen_apply(right_apply(back, inverse), screen_second)
    stacked = jnp.stack([image[0], image[1]])
    return (
        stacked.reshape(2, side_tiles, win_size, side_tiles, win_size)
        .transpose(1, 3, 0, 2, 4)
        .reshape(tile_count, width)
    )


def exchanged(strip, screen_first, screen_second, owners, live, place):
    win_size = strip.shape[1]
    sub_size = screen_first.shape[-1]
    side_tiles = sub_size // win_size
    tile_count = side_tiles * side_tiles
    width = 2 * win_size * win_size
    peer_count = lax.axis_size("facet")
    win_local = strip.shape[2] // win_size
    sub_local = SUB_DEV
    subgrid_count = sub_local * peer_count
    capacity = max(2, (7 * win_local + 2 * subgrid_count - 1) // (2 * subgrid_count))
    total_slots = subgrid_count * capacity
    small_real, small_imag = dft_table(win_size, -1.0)
    small = (small_real.astype(jnp.bfloat16), small_imag.astype(jnp.bfloat16))
    front = left_apply(small, (strip[0], strip[1]))
    contrib = jnp.stack([front[0], front[1]]).astype(jnp.bfloat16)
    windows = (
        contrib.reshape(2, win_size, win_local, win_size)
        .transpose(2, 0, 1, 3)
        .reshape(win_local, width)
    )
    flat_owner = owners[0].reshape(-1)
    flat_live = live[0].reshape(-1)
    flat_place = place[0].reshape(-1)
    entries = flat_owner.shape[0]
    order_index = jnp.arange(entries, dtype=jnp.int32)
    earlier = (flat_owner[:, None] == flat_owner[None, :]) & (
        order_index[None, :] < order_index[:, None]
    )
    rank = jnp.sum(earlier.astype(jnp.int32), axis=1)
    slot_of = flat_owner * capacity + rank
    slot_index = jnp.arange(total_slots, dtype=jnp.int32)
    hit_rows = ((slot_of[None, :] == slot_index[:, None]) & (flat_live[None, :] == 1)).astype(
        jnp.int32
    )
    hit_cols = ((slot_of[:, None] == slot_index[None, :]) & (flat_live[:, None] == 1)).astype(
        jnp.int32
    )
    codes = jnp.sum(hit_rows * (flat_place[None, :] + 1), axis=1) - 1
    packer = jnp.sum(hit_rows.reshape(total_slots, win_local, 3), axis=2).astype(jnp.bfloat16)
    unpacker = jnp.sum(hit_cols.reshape(win_local, 3, total_slots), axis=1).astype(jnp.bfloat16)
    outgoing = jnp.dot(packer, windows, preferred_element_type=jnp.float32).astype(jnp.bfloat16)
    outgoing = outgoing.reshape(peer_count, sub_local, capacity, width)
    codes = codes.reshape(peer_count, sub_local, capacity)
    big_real, big_imag = dft_table(sub_size, -1.0)
    forward = (big_real.astype(jnp.bfloat16), big_imag.astype(jnp.bfloat16))
    inverse = (big_real.astype(jnp.bfloat16), (-big_imag).astype(jnp.bfloat16))
    tile_index = jnp.arange(tile_count, dtype=jnp.int32)
    parcels = lax.all_to_all(outgoing, "facet", split_axis=0, concat_axis=0, tiled=True)
    labels = lax.all_to_all(codes, "facet", split_axis=0, concat_axis=0, tiled=True)
    item_count = parcels.shape[1]
    sources = parcels.shape[0]
    stacked = parcels.transpose(1, 0, 2, 3).reshape(item_count, sources * capacity, width)
    marks = labels.transpose(1, 0, 2).reshape(item_count, sources * capacity)

    def one_subgrid(pair):
        slabs, tags = pair
        embed_map = (tags[None, :] == tile_index[:, None]).astype(jnp.bfloat16)
        cut_map = (tags[:, None] == tile_index[None, :]).astype(jnp.bfloat16)
        tiles = jnp.dot(embed_map, slabs, preferred_element_type=jnp.float32).astype(jnp.bfloat16)
        finished = process_tiles(tiles, screen_first, screen_second, forward, inverse)
        return jnp.dot(cut_map, finished, preferred_element_type=jnp.float32).astype(jnp.bfloat16)

    result = lax.map(one_subgrid, (stacked, marks))
    returned = lax.all_to_all(
        result.reshape(item_count, sources, capacity, width).transpose(1, 0, 2, 3),
        "facet",
        split_axis=0,
        concat_axis=0,
        tiled=True,
    )
    summed = jnp.dot(
        unpacker, returned.reshape(total_slots, width), preferred_element_type=jnp.float32
    )
    field = (
        summed.reshape(win_local, 2, win_size, win_size)
        .transpose(1, 2, 0, 3)
        .reshape(2, win_size, win_local * win_size)
    )
    column = lax.psum_scatter(
        field.astype(jnp.bfloat16), "col", scatter_dimension=2, tiled=True
    ).astype(jnp.float32)
    back_real, back_imag = dft_table(win_size, 1.0)
    highest = lax.Precision.HIGHEST
    real = jnp.dot(back_real, column[0], precision=highest) - jnp.dot(
        back_imag, column[1], precision=highest
    )
    imag = jnp.dot(back_real, column[1], precision=highest) + jnp.dot(
        back_imag, column[0], precision=highest
    )
    return jnp.stack([real, imag])


GATHER_BYTES = 16 << 20
UNROLL = 4
WHOLE, EARLY, LATE = 0, 1, 2


def host_table(length):
    index = np.arange(length, dtype=np.int64)
    angle = (index[:, None] * index[None, :] % length) * (2.0 * math.pi / length)
    scale = 1.0 / math.sqrt(length)
    return np.cos(angle) * scale, -np.sin(angle) * scale


def rounded_pair(pair):
    return tuple(part.astype(jnp.bfloat16).astype(np.float64) for part in pair)


def left_block(real, imag):
    return np.concatenate(
        [np.concatenate([real, -imag], axis=1), np.concatenate([imag, real], axis=1)], axis=0
    )


def fill_blocks(front_ref, big_ref, first_ref, forward_ref, inverse_ref):
    half = big_ref.shape[1]
    low, high = pl.ds(0, half), pl.ds(half, half)
    first_ref[low, low] = front_ref[0]
    first_ref[low, high] = -front_ref[1]
    first_ref[high, low] = front_ref[1]
    first_ref[high, high] = front_ref[0]
    forward_ref[low, low] = big_ref[0]
    forward_ref[low, high] = big_ref[1]
    forward_ref[high, low] = -big_ref[1]
    forward_ref[high, high] = big_ref[0]
    inverse_ref[low, low] = big_ref[0]
    inverse_ref[low, high] = -big_ref[1]
    inverse_ref[high, low] = big_ref[1]
    inverse_ref[high, high] = big_ref[0]


def table_pairs(sub_size, win_size):
    big = rounded_pair(host_table(sub_size))
    small = rounded_pair(host_table(win_size))
    eye = np.eye(sub_size // win_size)
    wide = (np.kron(eye, small[0]), np.kron(eye, small[1]))
    front = (big[0] @ wide[0] - big[1] @ wide[1], big[0] @ wide[1] + big[1] @ wide[0])
    return np.stack(front).astype(jnp.bfloat16), np.stack(big).astype(jnp.bfloat16)


def meet(partners):
    barrier = pltpu.get_barrier_semaphore()
    for partner in partners:
        pl.semaphore_signal(
            barrier, inc=1, device_id=partner, device_id_type=pl.DeviceIdType.MESH
        )
    pl.semaphore_wait(barrier, len(partners))


def gather_body(
    peers,
    strip_ref,
    codes_ref,
    front_ref,
    big_ref,
    out_ref,
    all_codes_ref,
    first_out,
    forward_out,
    inverse_out,
    first_ref,
    forward_ref,
    inverse_ref,
    send_sem,
    recv_sem,
    code_send,
    code_recv,
    local_sem,
):
    levels = peers // 2
    facet, col = lax.axis_index("facet"), lax.axis_index("col")
    z, y = facet // 2, facet % 2
    x, core = col // 2, col % 2
    half = strip_ref.shape[1] // 2
    higher = [lax.rem(z + d, levels) for d in range(1, levels)]
    z_peers = [(level * 2 + y, col) for level in higher]
    y_peer = (z * 2 + 1 - y, col)
    x_peer = (facet, (1 - x) * 2 + core)
    core_peer = (facet, x * 2 + 1 - core)
    corners = [(level * 2 + 1 - y, col) for level in higher]
    meet(z_peers + [y_peer, x_peer, core_peer] + corners)
    sent = []

    def piece(ref, x_at, core_at, span):
        first = core_at * half + (half // 2 if span == LATE else 0)
        rows = half if span == WHOLE else half // 2
        return ref.at[x_at, pl.ds(pl.multiple_of(first, half // 2), rows)]

    def guarded(condition, action):
        if condition is None:
            action()
        else:
            pl.when(condition)(action)

    def send(condition, source, item, level, x_at, core_at, span, kind, lane, target):
        def describe():
            return pltpu.make_async_remote_copy(
                src_ref=piece(source, x_at, core_at, span),
                dst_ref=piece(out_ref.at[item], x_at, core_at, span),
                send_sem=send_sem.at[lane, level],
                recv_sem=recv_sem.at[kind, item],
                device_id=target,
                device_id_type=pl.DeviceIdType.MESH,
            )

        guarded(condition, lambda: describe().start())
        sent.append((condition, describe))

    def arrived(condition, item, x_at, core_at, span, kind):
        def wait():
            view = piece(out_ref.at[item], x_at, core_at, span)
            pltpu.make_async_copy(view, view, recv_sem.at[kind, item]).wait()

        guarded(condition, wait)

    def level_sets(distance):
        if distance == 0:
            return [(None, z, None, 0, None)]
        up = ((z + 1) * 2 + y, col)
        down = ((z - 1) * 2 + y, col)
        below, above = z - distance >= 0, z + distance < levels
        return [
            (below, z - distance, below & (z < levels - 1), 0, up),
            (above, z + distance, above & (z > 0), 1, down),
        ]

    send(None, strip_ref, facet, z, x, core, WHOLE, 0, 2, y_peer)
    send(z < levels - 1, strip_ref, facet, z, x, core, WHOLE, 0, 0, ((z + 1) * 2 + y, col))
    send(z > 0, strip_ref, facet, z, x, core, WHOLE, 0, 1, ((z - 1) * 2 + y, col))
    send(None, strip_ref, facet, z, 1 - x, core, EARLY, 4, 7, y_peer)
    codes_sent = []
    for number, target in enumerate([y_peer] + z_peers + corners):
        copy = pltpu.make_async_remote_copy(
            src_ref=codes_ref,
            dst_ref=all_codes_ref.at[facet],
            send_sem=code_send.at[number],
            recv_sem=code_recv.at[facet],
            device_id=target,
            device_id_type=pl.DeviceIdType.MESH,
        )
        copy.start()
        codes_sent.append(copy)
    kept = [
        pltpu.make_async_copy(strip_ref, out_ref.at[facet], local_sem.at[0]),
        pltpu.make_async_copy(codes_ref, all_codes_ref.at[facet], local_sem.at[1]),
    ]
    for copy in kept:
        copy.start()
    fill_blocks(front_ref, big_ref, first_ref, forward_ref, inverse_ref)
    for number, (source, target) in enumerate(
        [(first_ref, first_out), (forward_ref, forward_out), (inverse_ref, inverse_out)]
    ):
        copy = pltpu.make_async_copy(source, target, local_sem.at[2 + number])
        copy.start()
        kept.append(copy)

    def along_z(distance):
        for here, level, onward, lane, target in level_sets(distance):
            item = level * 2 + y
            source = out_ref.at[item]
            arrived(here, item, x, core, WHOLE, 0)
            send(onward, source, item, level, x, core, WHOLE, 0, lane, target)
            send(here, source, item, level, x, core, WHOLE, 0, 2, y_peer)
            send(here, source, item, level, x, core, WHOLE, 1, 3, x_peer)
            send(here, source, item, level, x, core, WHOLE, 2, 5, core_peer)

    def along_y(distance):
        for here, level, _, _, _ in level_sets(distance):
            item = level * 2 + 1 - y
            source = out_ref.at[item]
            arrived(here, item, x, core, WHOLE, 0)
            send(here, source, item, level, x, core, LATE, 1, 4, x_peer)
            send(here, source, item, level, x, core, WHOLE, 2, 6, core_peer)

    def along_x(distance):
        for here, level, _, _, _ in level_sets(distance):
            item = level * 2 + y
            source = out_ref.at[item]
            arrived(here, item, 1 - x, core, WHOLE, 1)
            send(here, source, item, level, 1 - x, core, EARLY, 4, 7, y_peer)
            send(here, source, item, level, 1 - x, core, WHOLE, 3, 8, core_peer)

    def corner(distance, span, kind, onward, lane):
        for here, level, _, _, _ in level_sets(distance):
            item = level * 2 + 1 - y
            arrived(here, item, 1 - x, core, span, kind)
            send(here, out_ref.at[item], item, level, 1 - x, core, span, onward, lane, core_peer)

    for distance in range(1, levels + 3):
        if distance < levels:
            along_z(distance)
        if 1 <= distance - 1 < levels:
            along_x(distance - 1)
        if 0 <= distance - 1 < levels:
            along_y(distance - 1)
        if 0 <= distance - 2 < levels:
            corner(distance - 2, LATE, 1, 3, 9)
            corner(distance - 2, EARLY, 4, 5, 10)
    for distance in range(levels):
        for here, level, _, _, _ in level_sets(distance):
            same, other = level * 2 + y, level * 2 + 1 - y
            if distance > 0:
                arrived(here, same, x, 1 - core, WHOLE, 2)
                arrived(here, same, 1 - x, 1 - core, WHOLE, 3)
            arrived(here, other, x, 1 - core, WHOLE, 2)
            arrived(here, other, 1 - x, 1 - core, LATE, 3)
            arrived(here, other, 1 - x, 1 - core, EARLY, 5)
    for item in [level * 2 + y for level in higher] + [z * 2 + 1 - y] + [
        level * 2 + 1 - y for level in higher
    ]:
        pltpu.make_async_copy(
            all_codes_ref.at[item], all_codes_ref.at[item], code_recv.at[item]
        ).wait()
    for condition, describe in sent:
        guarded(condition, lambda describe=describe: describe().wait_send())
    for copy in codes_sent:
        copy.wait_send()
    for copy in kept:
        copy.wait()


def gather_strips(strip, codes, peers, sub_size, win_size):
    front, big = table_pairs(sub_size, win_size)
    full = (2 * sub_size, 2 * sub_size)
    lanes = 128
    padded = jnp.pad(codes, ((0, 0), (0, lanes - codes.shape[1])), constant_values=-1)
    vmem = pl.BlockSpec(memory_space=pltpu.VMEM)
    anywhere = pl.BlockSpec(memory_space=pl.ANY)
    levels = peers // 2
    return pl.pallas_call(
        functools.partial(gather_body, peers),
        out_shape=[
            jax.ShapeDtypeStruct((peers,) + strip.shape, strip.dtype),
            jax.ShapeDtypeStruct((peers,) + padded.shape, padded.dtype),
        ]
        + [jax.ShapeDtypeStruct(full, jnp.bfloat16)] * 3,
        in_specs=[vmem] * 4,
        out_specs=[anywhere] * 5,
        scratch_shapes=[pltpu.VMEM(full, jnp.bfloat16)] * 3
        + [
            pltpu.SemaphoreType.DMA((11, levels)),
            pltpu.SemaphoreType.DMA((6, peers)),
            pltpu.SemaphoreType.DMA((peers,)),
            pltpu.SemaphoreType.DMA((peers,)),
            pltpu.SemaphoreType.DMA((5,)),
        ],
        compiler_params=pltpu.CompilerParams(collective_id=0, has_side_effects=True),
        name="gather",
    )(strip, padded, jnp.asarray(front), jnp.asarray(big))


def reduce_body(
    levels,
    partial_ref,
    out_ref,
    held,
    from_core,
    from_x_wide,
    from_y_wide,
    from_y,
    from_x,
    done,
    from_z,
    send_sem,
    recv_sem,
    z_send,
    z_recv,
    local_sem,
):
    facet, col = lax.axis_index("facet"), lax.axis_index("col")
    z, y = facet // 2, facet % 2
    x, core = col // 2, col % 2
    half = out_ref.shape[1] // 2
    top, bottom = pl.ds(0, half), pl.ds(half, half)
    order = [lax.rem(z + d, levels) for d in range(1, levels)] + [z]
    z_peers = [(level * 2 + y, col) for level in order[:-1]]
    y_peer = (z * 2 + 1 - y, col)
    x_peer = (facet, (1 - x) * 2 + core)
    core_peer = (facet, x * 2 + 1 - core)
    meet(z_peers + [y_peer, x_peer, core_peer])
    sent = []

    def send(source, target, kind, number, peer):
        copy = pltpu.make_async_remote_copy(
            src_ref=source,
            dst_ref=target,
            send_sem=send_sem.at[kind, number],
            recv_sem=recv_sem.at[kind, number],
            device_id=peer,
            device_id_type=pl.DeviceIdType.MESH,
        )
        copy.start()
        sent.append(copy)
        return copy

    def add(target, left, right):
        target[...] = (left[...].astype(jnp.float32) + right[...].astype(jnp.float32)).astype(
            target.dtype
        )

    first, kept = [], []
    for number, level in enumerate(order):
        first.append(
            send(partial_ref.at[1 - core, level], from_core.at[number], 0, number, core_peer)
        )
        copy = pltpu.make_async_copy(
            partial_ref.at[core, level], held.at[number], local_sem.at[number]
        )
        copy.start()
        kept.append(copy)
    wide_x, wide_y, narrow_x, narrow_y, across = [], [], [], [], []

    def join_cores(number):
        kept[number].wait()
        first[number].wait_recv()

        def body(index, carry):
            y_at, x_at, part = index // 4, index // 2 % 2, index % 2
            add(
                held.at[number, y_at, x_at, part],
                held.at[number, y_at, x_at, part],
                from_core.at[number, y_at, x_at, part],
            )
            return carry

        lax.fori_loop(0, 8, body, 0)
        wide_x.append(
            send(held.at[number, :, 1 - x, :, top], from_x_wide.at[number], 1, number, x_peer)
        )
        wide_y.append(
            send(held.at[number, 1 - y, :, :, bottom], from_y_wide.at[number], 2, number, y_peer)
        )

    def join_wide(number):
        wide_x[number].wait_recv()

        def body_x(index, carry):
            place = held.at[number, index // 2, x, index % 2, top]
            add(place, place, from_x_wide.at[number, index // 2, index % 2])
            return carry

        lax.fori_loop(0, 4, body_x, 0)
        narrow_y.append(
            send(held.at[number, 1 - y, x, :, top], from_y.at[number], 3, number, y_peer)
        )
        wide_y[number].wait_recv()

        def body_y(index, carry):
            place = held.at[number, y, index // 2, index % 2, bottom]
            add(place, place, from_y_wide.at[number, index // 2, index % 2])
            return carry

        lax.fori_loop(0, 4, body_y, 0)
        narrow_x.append(
            send(held.at[number, y, 1 - x, :, bottom], from_x.at[number], 4, number, x_peer)
        )

    def join_narrow(number):
        narrow_y[number].wait_recv()
        for part in range(2):
            add(
                done.at[number, part, top],
                held.at[number, y, x, part, top],
                from_y.at[number, part],
            )
        narrow_x[number].wait_recv()
        for part in range(2):
            add(
                done.at[number, part, bottom],
                held.at[number, y, x, part, bottom],
                from_x.at[number, part],
            )
        if number < levels - 1:
            copy = pltpu.make_async_remote_copy(
                src_ref=done.at[number],
                dst_ref=from_z.at[number],
                send_sem=z_send.at[number],
                recv_sem=z_recv.at[number],
                device_id=z_peers[number],
                device_id_type=pl.DeviceIdType.MESH,
            )
            copy.start()
            across.append(copy)

    for step in range(levels + 2):
        if step < levels:
            join_cores(step)
        if 0 <= step - 1 < levels:
            join_wide(step - 1)
        if 0 <= step - 2 < levels:
            join_narrow(step - 2)
    for copy in across:
        copy.wait_recv()
    for part in range(2):
        total = done[levels - 1, part].astype(jnp.float32)
        for number in range(levels - 1):
            total += from_z[number, part].astype(jnp.float32)
        out_ref[part] = total
    for copy in sent + across:
        copy.wait_send()


def reduce_partials(partial, levels, win_size, width):
    kind = partial.dtype
    half = win_size // 2
    return pl.pallas_call(
        functools.partial(reduce_body, levels),
        out_shape=jax.ShapeDtypeStruct((2, win_size, width), jnp.float32),
        in_specs=[pl.BlockSpec(memory_space=pl.ANY)],
        out_specs=pl.BlockSpec(memory_space=pltpu.VMEM),
        scratch_shapes=[
            pltpu.VMEM((levels, 2, 2, 2, win_size, width), kind),
            pltpu.VMEM((levels, 2, 2, 2, win_size, width), kind),
            pltpu.VMEM((levels, 2, 2, half, width), kind),
            pltpu.VMEM((levels, 2, 2, half, width), kind),
            pltpu.VMEM((levels, 2, half, width), kind),
            pltpu.VMEM((levels, 2, half, width), kind),
            pltpu.VMEM((levels, 2, win_size, width), kind),
            pltpu.VMEM((levels - 1, 2, win_size, width), kind),
            pltpu.SemaphoreType.DMA((5, levels)),
            pltpu.SemaphoreType.DMA((5, levels)),
            pltpu.SemaphoreType.DMA((levels - 1,)),
            pltpu.SemaphoreType.DMA((levels - 1,)),
            pltpu.SemaphoreType.DMA((levels,)),
        ],
        compiler_params=pltpu.CompilerParams(
            collective_id=1, has_side_effects=True, vmem_limit_bytes=58 << 20
        ),
        name="reduce",
    )(partial.reshape(2, levels, 2, 2, 2, win_size, width))


def parted(value, count):
    if count & (count - 1) == 0:
        return lax.shift_right_logical(value, count.bit_length() - 1), value & (count - 1)
    return lax.div(value, count), lax.rem(value, count)


def local_body(
    sub_local,
    capacity,
    codes_ref,
    strips_hbm,
    screen_first_hbm,
    screen_second_hbm,
    first_hbm,
    forward_hbm,
    inverse_hbm,
    out_hbm,
    strips_ref,
    screen_first_ref,
    screen_second_ref,
    first_ref,
    forward_ref,
    inverse_ref,
    out_ref,
    field,
    tall_all,
    flat,
    listed,
    strip_sem,
    table_sem,
    out_sem,
):
    peers = codes_ref.shape[0]
    win = strips_ref.shape[2]
    win_local = strips_ref.shape[3] // win
    size = screen_first_ref.shape[1]
    tiles = size // win
    pair = 2 * win
    part_windows = out_ref.shape[3] // win
    parts = out_ref.shape[0] // peers
    base = lax.axis_index("facet") * sub_local
    lane_half = lax.broadcasted_iota(jnp.int32, (win, pair), 1) // win
    step = size // 2
    loads = [
        pltpu.make_async_copy(strips_hbm.at[peer], strips_ref.at[peer], strip_sem.at[peer])
        for peer in range(peers)
    ]
    tables = [
        pltpu.make_async_copy(source, target, table_sem.at[number])
        for number, (source, target) in enumerate(
            [
                (first_hbm, first_ref),
                (forward_hbm, forward_ref),
                (screen_first_hbm, screen_first_ref),
                (inverse_hbm, inverse_ref),
                (screen_second_hbm, screen_second_ref),
            ]
        )
    ]
    for copy in loads + tables:
        copy.start()

    def zero_out(index, carry):
        out_ref[index] = jnp.zeros(out_ref.shape[1:], out_ref.dtype)
        return carry

    lax.fori_loop(0, out_ref.shape[0], zero_out, 0)

    def list_up(number):
        def peer_loop(peer, count):
            for slot in range(capacity):
                code = codes_ref[peer, base + number, slot]
                listed[number, count] = peer * (win_local * tiles * tiles) + code
                count += (code >= 0).astype(jnp.int32)
            return count

        count = lax.fori_loop(0, peers, peer_loop, 0)
        for extra in range(UNROLL):
            listed[number, count + extra] = -1
        return lax.div(count + UNROLL - 1, UNROLL)

    rounds = [list_up(number) for number in range(sub_local)]

    def entry(number, index):
        value = listed[number, index]
        code = jnp.maximum(value, 0)
        peer, rest = parted(code, win_local * tiles * tiles)
        window, spot = parted(rest, tiles * tiles)
        row, column = parted(spot, tiles)
        return value >= 0, peer, window, row, column

    def embed_all(number):
        field[...] = jnp.zeros(field.shape, field.dtype)

        def body(turn, carry):
            todo = []
            for extra in range(UNROLL):
                valid, peer, window, row, column = entry(number, turn * UNROLL + extra)
                at, odd = parted(window, 2)
                lanes = pl.ds(pl.multiple_of(at * pair, pair), pair)
                at, column_odd = parted(column, 2)
                target = pl.ds(pl.multiple_of(at * pair, pair), pair)
                chosen = lane_half == jnp.where(valid, column_odd, 2)
                shift = (odd ^ column_odd) * win
                for part in range(2):
                    piece = strips_ref[peer, part, :, lanes].astype(jnp.float32)
                    piece = jnp.where(chosen, pltpu.roll(piece, shift, 1), 0.0)
                    rows = pl.ds(pl.multiple_of(part * size + row * win, win), win)
                    todo.append((rows, target, piece))
            for rows, target, piece in todo:
                field[rows, target] += piece
            return carry

        lax.fori_loop(0, rounds[number], body, 0)
        tall_all[number] = field[...].astype(jnp.bfloat16)

    for copy in loads:
        copy.wait()
    for number in range(sub_local):
        embed_all(number)
    for copy in tables:
        copy.wait()

    def transform(number, carry):
        tall = tall_all.at[number]

        def left(table_ref):
            for part in range(2):
                for half in range(2):
                    rows = pl.ds(part * size + half * step, step)
                    flat[pl.ds(half * step, step), pl.ds(part * size, size)] = jnp.dot(
                        table_ref[rows, :], tall[...], preferred_element_type=jnp.float32
                    ).astype(jnp.bfloat16)

        def right(table_ref, screen_ref):
            for half in range(2):
                rows = pl.ds(half * step, step)
                product = jnp.dot(flat[rows, :], table_ref[...], preferred_element_type=jnp.float32)
                real_part, imag_part = product[:, :size], product[:, size:]
                screen_real = screen_ref[0, rows, :].astype(jnp.float32)
                screen_imag = screen_ref[1, rows, :].astype(jnp.float32)
                tall[rows, :] = (real_part * screen_real - imag_part * screen_imag).astype(
                    jnp.bfloat16
                )
                tall[pl.ds(size + half * step, step), :] = (
                    real_part * screen_imag + imag_part * screen_real
                ).astype(jnp.bfloat16)

        left(first_ref)
        right(forward_ref, screen_first_ref)
        left(forward_ref)
        right(inverse_ref, screen_second_ref)
        return carry

    lax.fori_loop(0, sub_local, transform, 0)

    def cut_all(number):
        def body(turn, carry):
            todo = []
            for extra in range(UNROLL):
                valid, peer, window, row, column = entry(number, turn * UNROLL + extra)
                at, column_odd = parted(column, 2)
                source = pl.ds(pl.multiple_of(at * pair, pair), pair)
                part_index, spot = parted(window, part_windows)
                at, odd = parted(spot, 2)
                lanes = pl.ds(pl.multiple_of(at * pair, pair), pair)
                outer, inner = parted(part_index, 2)
                slab = (inner * peers + peer) * (parts // 2) + outer
                chosen = lane_half == jnp.where(valid, odd, 2)
                shift = (odd ^ column_odd) * win
                for part in range(2):
                    rows = pl.ds(pl.multiple_of(part * size + row * win, win), win)
                    piece = tall_all[number, rows, source].astype(jnp.float32)
                    piece = jnp.where(chosen, pltpu.roll(piece, shift, 1), 0.0)
                    todo.append((slab, part, lanes, piece))
            for slab, part, lanes, piece in todo:
                held = out_ref[slab, part, :, lanes].astype(jnp.float32)
                out_ref[slab, part, :, lanes] = (held + piece).astype(out_ref.dtype)
            return carry

        lax.fori_loop(0, rounds[number], body, 0)

    for number in range(sub_local):
        cut_all(number)
    copy = pltpu.make_async_copy(out_ref, out_hbm, out_sem)
    copy.start()
    copy.wait()


def entry_codes(owners, live, place, subgrid_count, tile_count):
    win_local = owners.shape[1]
    capacity = max(2, (7 * win_local + 2 * subgrid_count - 1) // (2 * subgrid_count))
    owner = owners[0].reshape(-1)
    count = owner.shape[0]
    window = jnp.arange(count, dtype=jnp.int32) // 3
    label = window * tile_count + place[0].reshape(-1) + 1
    order = jnp.arange(count, dtype=jnp.int32)
    earlier = (owner[:, None] == owner[None, :]) & (order[None, :] < order[:, None])
    rank = jnp.sum(earlier.astype(jnp.int32), axis=1)
    slot = jnp.where(live[0].reshape(-1) == 1, owner * capacity + rank, -1)
    slots = jnp.arange(subgrid_count * capacity, dtype=jnp.int32)
    hit = slot[None, :] == slots[:, None]
    codes = jnp.sum(jnp.where(hit, label[None, :], 0), axis=1) - 1
    return codes.reshape(subgrid_count, capacity)


def gathered(strip, screen_first, screen_second, owners, live, place):
    win_size = strip.shape[1]
    sub_size = screen_first.shape[-1]
    tile_count = (sub_size // win_size) ** 2
    peer_count = lax.axis_size("facet")
    parts = lax.axis_size("col")
    sub_local = SUB_DEV
    codes = entry_codes(owners, live, place, sub_local * peer_count, tile_count)
    capacity = codes.shape[1]
    strips, codes, first, forward, inverse = gather_strips(
        strip, codes, peer_count, sub_size, win_size
    )
    piece = strip.shape[2] // parts
    anywhere = pl.BlockSpec(memory_space=pl.ANY)
    slabs = (peer_count * parts, 2, win_size, piece)
    listing = -(-(peer_count * capacity + UNROLL) // 128) * 128
    partial = pl.pallas_call(
        functools.partial(local_body, sub_local, capacity),
        out_shape=jax.ShapeDtypeStruct(slabs, jnp.bfloat16),
        in_specs=[pl.BlockSpec(memory_space=pltpu.SMEM)] + [anywhere] * 6,
        out_specs=anywhere,
        scratch_shapes=[
            pltpu.VMEM(array.shape, array.dtype)
            for array in (strips, screen_first, screen_second, first, forward, inverse)
        ]
        + [
            pltpu.VMEM(slabs, jnp.bfloat16),
            pltpu.VMEM((2 * sub_size, sub_size), jnp.float32),
            pltpu.VMEM((sub_local, 2 * sub_size, sub_size), jnp.bfloat16),
            pltpu.VMEM((sub_size, 2 * sub_size), jnp.bfloat16),
            pltpu.SMEM((sub_local, listing), jnp.int32),
            pltpu.SemaphoreType.DMA((peer_count,)),
            pltpu.SemaphoreType.DMA((5,)),
            pltpu.SemaphoreType.DMA,
        ],
        compiler_params=pltpu.CompilerParams(vmem_limit_bytes=60 << 20),
        name="local",
    )(codes, strips, screen_first, screen_second, first, forward, inverse)
    mine = reduce_partials(partial, peer_count // 2, win_size, piece)
    return finish(mine.reshape(2 * win_size, piece), win_size)


def finish(mine, win_size):
    real, imag = host_table(win_size)
    table = jnp.asarray(left_block(real, -imag).astype(np.float32))
    image = jnp.dot(table, mine, precision=lax.Precision.HIGHEST)
    return image.reshape(2, win_size, mine.shape[1])


def shards(strip, screen_first, screen_second, owners, live, place):
    paired = lax.axis_size("facet") % 2 == 0 and lax.axis_size("col") == 4
    if paired and strip.size * strip.dtype.itemsize * lax.axis_size("facet") <= GATHER_BYTES:
        return gathered(strip, screen_first, screen_second, owners, live, place)
    return exchanged(strip, screen_first, screen_second, owners, live, place)


def solution(mesh):
    placed = (
        P(None, None, "facet"),
        P(),
        P(),
        P("col", "facet", None),
        P("col", "facet", None),
        P("col", "facet", None),
    )
    return jax.shard_map(
        shards,
        mesh=mesh,
        in_specs=placed,
        out_specs=P(None, None, ("facet", "col")),
        check_vma=False,
    )
```

```python
import math

import functools

import jax
import jax.numpy as jnp
import numpy as np
from jax import lax
from jax.experimental import pallas as pl
from jax.experimental.pallas import tpu as pltpu
from jax.sharding import PartitionSpec as P

SUB_DEV = 2


def dft_table(length, direction):
    index = jnp.arange(length, dtype=jnp.int32)
    phase = index[:, None] * index[None, :] % length
    angle = phase.astype(jnp.float32) * (2.0 * math.pi / length)
    scale = 1.0 / math.sqrt(length)
    return (jnp.cos(angle) * scale, direction * jnp.sin(angle) * scale)


def left_apply(table, field):
    real_table, imag_table = table
    real_part, imag_part = field
    real = jnp.dot(real_table, real_part, preferred_element_type=jnp.float32) - jnp.dot(
        imag_table, imag_part, preferred_element_type=jnp.float32
    )
    imag = jnp.dot(real_table, imag_part, preferred_element_type=jnp.float32) + jnp.dot(
        imag_table, real_part, preferred_element_type=jnp.float32
    )
    return (real, imag)


def right_apply(field, table):
    real_table, imag_table = table
    real_part, imag_part = field
    real = jnp.dot(real_part, real_table, preferred_element_type=jnp.float32) - jnp.dot(
        imag_part, imag_table, preferred_element_type=jnp.float32
    )
    imag = jnp.dot(real_part, imag_table, preferred_element_type=jnp.float32) + jnp.dot(
        imag_part, real_table, preferred_element_type=jnp.float32
    )
    return (real, imag)


def screen_apply(field, screen):
    real_part, imag_part = field
    screen_real = screen[0].astype(jnp.float32)
    screen_imag = screen[1].astype(jnp.float32)
    real = real_part * screen_real - imag_part * screen_imag
    imag = real_part * screen_imag + imag_part * screen_real
    return (real.astype(jnp.bfloat16), imag.astype(jnp.bfloat16))


def process_tiles(tiles, screen_first, screen_second, forward, inverse):
    tile_count, width = tiles.shape
    side_tiles = math.isqrt(tile_count)
    win_size = math.isqrt(width // 2)
    sub_size = side_tiles * win_size
    field = (
        tiles.reshape(side_tiles, side_tiles, 2, win_size, win_size)
        .transpose(2, 0, 3, 1, 4)
        .reshape(2, sub_size, sub_size)
    )
    rows = left_apply(forward, (field[0], field[1]))
    rows = (rows[0].astype(jnp.bfloat16), rows[1].astype(jnp.bfloat16))
    spectrum = screen_apply(right_apply(rows, forward), screen_first)
    back = left_apply(inverse, spectrum)
    back = (back[0].astype(jnp.bfloat16), back[1].astype(jnp.bfloat16))
    image = screen_apply(right_apply(back, inverse), screen_second)
    stacked = jnp.stack([image[0], image[1]])
    return (
        stacked.reshape(2, side_tiles, win_size, side_tiles, win_size)
        .transpose(1, 3, 0, 2, 4)
        .reshape(tile_count, width)
    )


def exchanged(strip, screen_first, screen_second, owners, live, place):
    win_size = strip.shape[1]
    sub_size = screen_first.shape[-1]
    side_tiles = sub_size // win_size
    tile_count = side_tiles * side_tiles
    width = 2 * win_size * win_size
    peer_count = lax.axis_size("facet")
    win_local = strip.shape[2] // win_size
    sub_local = SUB_DEV
    subgrid_count = sub_local * peer_count
    capacity = max(2, (7 * win_local + 2 * subgrid_count - 1) // (2 * subgrid_count))
    total_slots = subgrid_count * capacity
    small_real, small_imag = dft_table(win_size, -1.0)
    small = (small_real.astype(jnp.bfloat16), small_imag.astype(jnp.bfloat16))
    front = left_apply(small, (strip[0], strip[1]))
    contrib = jnp.stack([front[0], front[1]]).astype(jnp.bfloat16)
    windows = (
        contrib.reshape(2, win_size, win_local, win_size)
        .transpose(2, 0, 1, 3)
        .reshape(win_local, width)
    )
    flat_owner = owners[0].reshape(-1)
    flat_live = live[0].reshape(-1)
    flat_place = place[0].reshape(-1)
    entries = flat_owner.shape[0]
    order_index = jnp.arange(entries, dtype=jnp.int32)
    earlier = (flat_owner[:, None] == flat_owner[None, :]) & (
        order_index[None, :] < order_index[:, None]
    )
    rank = jnp.sum(earlier.astype(jnp.int32), axis=1)
    slot_of = flat_owner * capacity + rank
    slot_index = jnp.arange(total_slots, dtype=jnp.int32)
    hit_rows = ((slot_of[None, :] == slot_index[:, None]) & (flat_live[None, :] == 1)).astype(
        jnp.int32
    )
    hit_cols = ((slot_of[:, None] == slot_index[None, :]) & (flat_live[:, None] == 1)).astype(
        jnp.int32
    )
    codes = jnp.sum(hit_rows * (flat_place[None, :] + 1), axis=1) - 1
    packer = jnp.sum(hit_rows.reshape(total_slots, win_local, 3), axis=2).astype(jnp.bfloat16)
    unpacker = jnp.sum(hit_cols.reshape(win_local, 3, total_slots), axis=1).astype(jnp.bfloat16)
    outgoing = jnp.dot(packer, windows, preferred_element_type=jnp.float32).astype(jnp.bfloat16)
    outgoing = outgoing.reshape(peer_count, sub_local, capacity, width)
    codes = codes.reshape(peer_count, sub_local, capacity)
    big_real, big_imag = dft_table(sub_size, -1.0)
    forward = (big_real.astype(jnp.bfloat16), big_imag.astype(jnp.bfloat16))
    inverse = (big_real.astype(jnp.bfloat16), (-big_imag).astype(jnp.bfloat16))
    tile_index = jnp.arange(tile_count, dtype=jnp.int32)
    parcels = lax.all_to_all(outgoing, "facet", split_axis=0, concat_axis=0, tiled=True)
    labels = lax.all_to_all(codes, "facet", split_axis=0, concat_axis=0, tiled=True)
    item_count = parcels.shape[1]
    sources = parcels.shape[0]
    stacked = parcels.transpose(1, 0, 2, 3).reshape(item_count, sources * capacity, width)
    marks = labels.transpose(1, 0, 2).reshape(item_count, sources * capacity)

    def one_subgrid(pair):
        slabs, tags = pair
        embed_map = (tags[None, :] == tile_index[:, None]).astype(jnp.bfloat16)
        cut_map = (tags[:, None] == tile_index[None, :]).astype(jnp.bfloat16)
        tiles = jnp.dot(embed_map, slabs, preferred_element_type=jnp.float32).astype(jnp.bfloat16)
        finished = process_tiles(tiles, screen_first, screen_second, forward, inverse)
        return jnp.dot(cut_map, finished, preferred_element_type=jnp.float32).astype(jnp.bfloat16)

    result = lax.map(one_subgrid, (stacked, marks))
    returned = lax.all_to_all(
        result.reshape(item_count, sources, capacity, width).transpose(1, 0, 2, 3),
        "facet",
        split_axis=0,
        concat_axis=0,
        tiled=True,
    )
    summed = jnp.dot(
        unpacker, returned.reshape(total_slots, width), preferred_element_type=jnp.float32
    )
    field = (
        summed.reshape(win_local, 2, win_size, win_size)
        .transpose(1, 2, 0, 3)
        .reshape(2, win_size, win_local * win_size)
    )
    column = lax.psum_scatter(
        field.astype(jnp.bfloat16), "col", scatter_dimension=2, tiled=True
    ).astype(jnp.float32)
    back_real, back_imag = dft_table(win_size, 1.0)
    highest = lax.Precision.HIGHEST
    real = jnp.dot(back_real, column[0], precision=highest) - jnp.dot(
        back_imag, column[1], precision=highest
    )
    imag = jnp.dot(back_real, column[1], precision=highest) + jnp.dot(
        back_imag, column[0], precision=highest
    )
    return jnp.stack([real, imag])


GATHER_BYTES = 16 << 20
UNROLL = 8
WHOLE, EARLY, LATE = 0, 1, 2


def host_table(length):
    index = np.arange(length, dtype=np.int64)
    angle = (index[:, None] * index[None, :] % length) * (2.0 * math.pi / length)
    scale = 1.0 / math.sqrt(length)
    return np.cos(angle) * scale, -np.sin(angle) * scale


def rounded_pair(pair):
    return tuple(part.astype(jnp.bfloat16).astype(np.float64) for part in pair)


def left_block(real, imag):
    return np.concatenate(
        [np.concatenate([real, -imag], axis=1), np.concatenate([imag, real], axis=1)], axis=0
    )


def fill_blocks(front_ref, big_ref, first_ref, forward_ref, inverse_ref):
    half = big_ref.shape[1]
    low, high = pl.ds(0, half), pl.ds(half, half)
    first_ref[low, low] = front_ref[0]
    first_ref[low, high] = -front_ref[1]
    first_ref[high, low] = front_ref[1]
    first_ref[high, high] = front_ref[0]
    forward_ref[low, low] = big_ref[0]
    forward_ref[low, high] = big_ref[1]
    forward_ref[high, low] = -big_ref[1]
    forward_ref[high, high] = big_ref[0]
    inverse_ref[low, low] = big_ref[0]
    inverse_ref[low, high] = -big_ref[1]
    inverse_ref[high, low] = big_ref[1]
    inverse_ref[high, high] = big_ref[0]


def table_pairs(sub_size, win_size):
    big = rounded_pair(host_table(sub_size))
    small = rounded_pair(host_table(win_size))
    eye = np.eye(sub_size // win_size)
    wide = (np.kron(eye, small[0]), np.kron(eye, small[1]))
    front = (big[0] @ wide[0] - big[1] @ wide[1], big[0] @ wide[1] + big[1] @ wide[0])
    return np.stack(front).astype(jnp.bfloat16), np.stack(big).astype(jnp.bfloat16)


def meet(partners):
    barrier = pltpu.get_barrier_semaphore()
    for partner in partners:
        pl.semaphore_signal(
            barrier, inc=1, device_id=partner, device_id_type=pl.DeviceIdType.MESH
        )
    pl.semaphore_wait(barrier, len(partners))


def gather_body(
    peers,
    strip_ref,
    codes_ref,
    front_ref,
    big_ref,
    out_ref,
    all_codes_ref,
    first_out,
    forward_out,
    inverse_out,
    first_ref,
    forward_ref,
    inverse_ref,
    send_sem,
    recv_sem,
    code_send,
    code_recv,
    local_sem,
):
    levels = peers // 2
    facet, col = lax.axis_index("facet"), lax.axis_index("col")
    z, y = facet // 2, facet % 2
    x, core = col // 2, col % 2
    half = strip_ref.shape[1] // 2
    higher = [lax.rem(z + d, levels) for d in range(1, levels)]
    z_peers = [(level * 2 + y, col) for level in higher]
    y_peer = (z * 2 + 1 - y, col)
    x_peer = (facet, (1 - x) * 2 + core)
    core_peer = (facet, x * 2 + 1 - core)
    corners = [(level * 2 + 1 - y, col) for level in higher]
    meet(z_peers + [y_peer, x_peer, core_peer] + corners)
    sent = []

    def piece(ref, x_at, core_at, span):
        first = core_at * half + (half // 2 if span == LATE else 0)
        rows = half if span == WHOLE else half // 2
        return ref.at[x_at, pl.ds(pl.multiple_of(first, half // 2), rows)]

    def guarded(condition, action):
        if condition is None:
            action()
        else:
            pl.when(condition)(action)

    def send(condition, source, item, level, x_at, core_at, span, kind, lane, target):
        def describe():
            return pltpu.make_async_remote_copy(
                src_ref=piece(source, x_at, core_at, span),
                dst_ref=piece(out_ref.at[item], x_at, core_at, span),
                send_sem=send_sem.at[lane, level],
                recv_sem=recv_sem.at[kind, item],
                device_id=target,
                device_id_type=pl.DeviceIdType.MESH,
            )

        guarded(condition, lambda: describe().start())
        sent.append((condition, describe))

    def arrived(condition, item, x_at, core_at, span, kind):
        def wait():
            view = piece(out_ref.at[item], x_at, core_at, span)
            pltpu.make_async_copy(view, view, recv_sem.at[kind, item]).wait()

        guarded(condition, wait)

    def level_sets(distance):
        if distance == 0:
            return [(None, z, None, 0, None)]
        up = ((z + 1) * 2 + y, col)
        down = ((z - 1) * 2 + y, col)
        below, above = z - distance >= 0, z + distance < levels
        return [
            (below, z - distance, below & (z < levels - 1), 0, up),
            (above, z + distance, above & (z > 0), 1, down),
        ]

    send(None, strip_ref, facet, z, x, core, WHOLE, 0, 2, y_peer)
    send(z < levels - 1, strip_ref, facet, z, x, core, WHOLE, 0, 0, ((z + 1) * 2 + y, col))
    send(z > 0, strip_ref, facet, z, x, core, WHOLE, 0, 1, ((z - 1) * 2 + y, col))
    send(None, strip_ref, facet, z, 1 - x, core, EARLY, 4, 7, y_peer)
    codes_sent = []
    for number, target in enumerate([y_peer] + z_peers + corners):
        copy = pltpu.make_async_remote_copy(
            src_ref=codes_ref,
            dst_ref=all_codes_ref.at[facet],
            send_sem=code_send.at[number],
            recv_sem=code_recv.at[facet],
            device_id=target,
            device_id_type=pl.DeviceIdType.MESH,
        )
        copy.start()
        codes_sent.append(copy)
    kept = [
        pltpu.make_async_copy(strip_ref, out_ref.at[facet], local_sem.at[0]),
        pltpu.make_async_copy(codes_ref, all_codes_ref.at[facet], local_sem.at[1]),
    ]
    for copy in kept:
        copy.start()
    fill_blocks(front_ref, big_ref, first_ref, forward_ref, inverse_ref)
    for number, (source, target) in enumerate(
        [(first_ref, first_out), (forward_ref, forward_out), (inverse_ref, inverse_out)]
    ):
        copy = pltpu.make_async_copy(source, target, local_sem.at[2 + number])
        copy.start()
        kept.append(copy)

    def along_z(distance):
        for here, level, onward, lane, target in level_sets(distance):
            item = level * 2 + y
            source = out_ref.at[item]
            arrived(here, item, x, core, WHOLE, 0)
            send(onward, source, item, level, x, core, WHOLE, 0, lane, target)
            send(here, source, item, level, x, core, WHOLE, 0, 2, y_peer)
            send(here, source, item, level, x, core, WHOLE, 1, 3, x_peer)
            send(here, source, item, level, x, core, WHOLE, 2, 5, core_peer)

    def along_y(distance):
        for here, level, _, _, _ in level_sets(distance):
            item = level * 2 + 1 - y
            source = out_ref.at[item]
            arrived(here, item, x, core, WHOLE, 0)
            send(here, source, item, level, x, core, LATE, 1, 4, x_peer)
            send(here, source, item, level, x, core, WHOLE, 2, 6, core_peer)

    def along_x(distance):
        for here, level, _, _, _ in level_sets(distance):
            item = level * 2 + y
            source = out_ref.at[item]
            arrived(here, item, 1 - x, core, WHOLE, 1)
            send(here, source, item, level, 1 - x, core, EARLY, 4, 7, y_peer)
            send(here, source, item, level, 1 - x, core, WHOLE, 3, 8, core_peer)

    def corner(distance, span, kind, onward, lane):
        for here, level, _, _, _ in level_sets(distance):
            item = level * 2 + 1 - y
            arrived(here, item, 1 - x, core, span, kind)
            send(here, out_ref.at[item], item, level, 1 - x, core, span, onward, lane, core_peer)

    for distance in range(1, levels + 3):
        if distance < levels:
            along_z(distance)
        if 1 <= distance - 1 < levels:
            along_x(distance - 1)
        if 0 <= distance - 1 < levels:
            along_y(distance - 1)
        if 0 <= distance - 2 < levels:
            corner(distance - 2, LATE, 1, 3, 9)
            corner(distance - 2, EARLY, 4, 5, 10)
    for distance in range(levels):
        for here, level, _, _, _ in level_sets(distance):
            same, other = level * 2 + y, level * 2 + 1 - y
            if distance > 0:
                arrived(here, same, x, 1 - core, WHOLE, 2)
                arrived(here, same, 1 - x, 1 - core, WHOLE, 3)
            arrived(here, other, x, 1 - core, WHOLE, 2)
            arrived(here, other, 1 - x, 1 - core, LATE, 3)
            arrived(here, other, 1 - x, 1 - core, EARLY, 5)
    for item in [level * 2 + y for level in higher] + [z * 2 + 1 - y] + [
        level * 2 + 1 - y for level in higher
    ]:
        pltpu.make_async_copy(
            all_codes_ref.at[item], all_codes_ref.at[item], code_recv.at[item]
        ).wait()
    for condition, describe in sent:
        guarded(condition, lambda describe=describe: describe().wait_send())
    for copy in codes_sent:
        copy.wait_send()
    for copy in kept:
        copy.wait()


def gather_strips(strip, codes, peers, sub_size, win_size):
    front, big = table_pairs(sub_size, win_size)
    full = (2 * sub_size, 2 * sub_size)
    lanes = 128
    padded = jnp.pad(codes, ((0, 0), (0, lanes - codes.shape[1])), constant_values=-1)
    vmem = pl.BlockSpec(memory_space=pltpu.VMEM)
    anywhere = pl.BlockSpec(memory_space=pl.ANY)
    levels = peers // 2
    return pl.pallas_call(
        functools.partial(gather_body, peers),
        out_shape=[
            jax.ShapeDtypeStruct((peers,) + strip.shape, strip.dtype),
            jax.ShapeDtypeStruct((peers,) + padded.shape, padded.dtype),
        ]
        + [jax.ShapeDtypeStruct(full, jnp.bfloat16)] * 3,
        in_specs=[vmem] * 4,
        out_specs=[anywhere] * 5,
        scratch_shapes=[pltpu.VMEM(full, jnp.bfloat16)] * 3
        + [
            pltpu.SemaphoreType.DMA((11, levels)),
            pltpu.SemaphoreType.DMA((6, peers)),
            pltpu.SemaphoreType.DMA((peers,)),
            pltpu.SemaphoreType.DMA((peers,)),
            pltpu.SemaphoreType.DMA((5,)),
        ],
        compiler_params=pltpu.CompilerParams(collective_id=0, has_side_effects=True),
        name="gather",
    )(strip, padded, jnp.asarray(front), jnp.asarray(big))


def reduce_body(
    levels,
    partial_ref,
    out_ref,
    held,
    from_core,
    from_x_wide,
    from_y_wide,
    from_y,
    from_x,
    done,
    from_z,
    send_sem,
    recv_sem,
    z_send,
    z_recv,
    local_sem,
):
    facet, col = lax.axis_index("facet"), lax.axis_index("col")
    z, y = facet // 2, facet % 2
    x, core = col // 2, col % 2
    half = out_ref.shape[1] // 2
    top, bottom = pl.ds(0, half), pl.ds(half, half)
    order = [lax.rem(z + d, levels) for d in range(1, levels)] + [z]
    z_peers = [(level * 2 + y, col) for level in order[:-1]]
    y_peer = (z * 2 + 1 - y, col)
    x_peer = (facet, (1 - x) * 2 + core)
    core_peer = (facet, x * 2 + 1 - core)
    meet(z_peers + [y_peer, x_peer, core_peer])
    sent = []

    def send(source, target, kind, number, peer):
        copy = pltpu.make_async_remote_copy(
            src_ref=source,
            dst_ref=target,
            send_sem=send_sem.at[kind, number],
            recv_sem=recv_sem.at[kind, number],
            device_id=peer,
            device_id_type=pl.DeviceIdType.MESH,
        )
        copy.start()
        sent.append(copy)
        return copy

    def add(target, left, right):
        target[...] = (left[...].astype(jnp.float32) + right[...].astype(jnp.float32)).astype(
            target.dtype
        )

    first, kept = [], []
    for number, level in enumerate(order):
        first.append(
            send(partial_ref.at[1 - core, level], from_core.at[number], 0, number, core_peer)
        )
        copy = pltpu.make_async_copy(
            partial_ref.at[core, level], held.at[number], local_sem.at[number]
        )
        copy.start()
        kept.append(copy)
    wide_x, wide_y, narrow_x, narrow_y, across = [], [], [], [], []

    def join_cores(number):
        kept[number].wait()
        first[number].wait_recv()

        def body(index, carry):
            y_at, x_at, part = index // 4, index // 2 % 2, index % 2
            add(
                held.at[number, y_at, x_at, part],
                held.at[number, y_at, x_at, part],
                from_core.at[number, y_at, x_at, part],
            )
            return carry

        lax.fori_loop(0, 8, body, 0)
        wide_x.append(
            send(held.at[number, :, 1 - x, :, top], from_x_wide.at[number], 1, number, x_peer)
        )
        wide_y.append(
            send(held.at[number, 1 - y, :, :, bottom], from_y_wide.at[number], 2, number, y_peer)
        )

    def join_wide(number):
        wide_x[number].wait_recv()

        def body_x(index, carry):
            place = held.at[number, index // 2, x, index % 2, top]
            add(place, place, from_x_wide.at[number, index // 2, index % 2])
            return carry

        lax.fori_loop(0, 4, body_x, 0)
        narrow_y.append(
            send(held.at[number, 1 - y, x, :, top], from_y.at[number], 3, number, y_peer)
        )
        wide_y[number].wait_recv()

        def body_y(index, carry):
            place = held.at[number, y, index // 2, index % 2, bottom]
            add(place, place, from_y_wide.at[number, index // 2, index % 2])
            return carry

        lax.fori_loop(0, 4, body_y, 0)
        narrow_x.append(
            send(held.at[number, y, 1 - x, :, bottom], from_x.at[number], 4, number, x_peer)
        )

    def join_narrow(number):
        narrow_y[number].wait_recv()
        for part in range(2):
            add(
                done.at[number, part, top],
                held.at[number, y, x, part, top],
                from_y.at[number, part],
            )
        narrow_x[number].wait_recv()
        for part in range(2):
            add(
                done.at[number, part, bottom],
                held.at[number, y, x, part, bottom],
                from_x.at[number, part],
            )
        if number < levels - 1:
            copy = pltpu.make_async_remote_copy(
                src_ref=done.at[number],
                dst_ref=from_z.at[number],
                send_sem=z_send.at[number],
                recv_sem=z_recv.at[number],
                device_id=z_peers[number],
                device_id_type=pl.DeviceIdType.MESH,
            )
            copy.start()
            across.append(copy)

    for step in range(levels + 2):
        if step < levels:
            join_cores(step)
        if 0 <= step - 1 < levels:
            join_wide(step - 1)
        if 0 <= step - 2 < levels:
            join_narrow(step - 2)
    for copy in across:
        copy.wait_recv()
    for part in range(2):
        total = done[levels - 1, part].astype(jnp.float32)
        for number in range(levels - 1):
            total += from_z[number, part].astype(jnp.float32)
        out_ref[part] = total
    for copy in sent + across:
        copy.wait_send()


def reduce_partials(partial, levels, win_size, width):
    kind = partial.dtype
    half = win_size // 2
    return pl.pallas_call(
        functools.partial(reduce_body, levels),
        out_shape=jax.ShapeDtypeStruct((2, win_size, width), jnp.float32),
        in_specs=[pl.BlockSpec(memory_space=pl.ANY)],
        out_specs=pl.BlockSpec(memory_space=pltpu.VMEM),
        scratch_shapes=[
            pltpu.VMEM((levels, 2, 2, 2, win_size, width), kind),
            pltpu.VMEM((levels, 2, 2, 2, win_size, width), kind),
            pltpu.VMEM((levels, 2, 2, half, width), kind),
            pltpu.VMEM((levels, 2, 2, half, width), kind),
            pltpu.VMEM((levels, 2, half, width), kind),
            pltpu.VMEM((levels, 2, half, width), kind),
            pltpu.VMEM((levels, 2, win_size, width), kind),
            pltpu.VMEM((levels - 1, 2, win_size, width), kind),
            pltpu.SemaphoreType.DMA((5, levels)),
            pltpu.SemaphoreType.DMA((5, levels)),
            pltpu.SemaphoreType.DMA((levels - 1,)),
            pltpu.SemaphoreType.DMA((levels - 1,)),
            pltpu.SemaphoreType.DMA((levels,)),
        ],
        compiler_params=pltpu.CompilerParams(
            collective_id=1, has_side_effects=True, vmem_limit_bytes=58 << 20
        ),
        name="reduce",
    )(partial.reshape(2, levels, 2, 2, 2, win_size, width))


def parted(value, count):
    if count & (count - 1) == 0:
        return lax.shift_right_logical(value, count.bit_length() - 1), value & (count - 1)
    return lax.div(value, count), lax.rem(value, count)


def local_body(
    sub_local,
    capacity,
    codes_ref,
    strips_hbm,
    screen_first_hbm,
    screen_second_hbm,
    first_hbm,
    forward_hbm,
    inverse_hbm,
    out_hbm,
    strips_ref,
    screen_first_ref,
    screen_second_ref,
    first_ref,
    forward_ref,
    inverse_ref,
    out_ref,
    field,
    tall_all,
    flat,
    listed,
    strip_sem,
    table_sem,
    out_sem,
):
    peers = codes_ref.shape[0]
    win = strips_ref.shape[2]
    win_local = strips_ref.shape[3] // win
    size = screen_first_ref.shape[1]
    tiles = size // win
    pair = 2 * win
    part_windows = out_ref.shape[3] // win
    parts = out_ref.shape[0] // peers
    base = lax.axis_index("facet") * sub_local
    lane_half = lax.broadcasted_iota(jnp.int32, (win, pair), 1) // win
    step = size
    loads = [
        pltpu.make_async_copy(strips_hbm.at[peer], strips_ref.at[peer], strip_sem.at[peer])
        for peer in range(peers)
    ]
    tables = [
        pltpu.make_async_copy(source, target, table_sem.at[number])
        for number, (source, target) in enumerate(
            [
                (first_hbm, first_ref),
                (forward_hbm, forward_ref),
                (screen_first_hbm, screen_first_ref),
                (inverse_hbm, inverse_ref),
                (screen_second_hbm, screen_second_ref),
            ]
        )
    ]
    for copy in loads + tables:
        copy.start()

    def zero_out(index, carry):
        out_ref[index] = jnp.zeros(out_ref.shape[1:], out_ref.dtype)
        return carry

    lax.fori_loop(0, out_ref.shape[0], zero_out, 0)

    def list_up(number):
        def peer_loop(peer, count):
            for slot in range(capacity):
                code = codes_ref[peer, base + number, slot]
                listed[number, count] = peer * (win_local * tiles * tiles) + code
                count += (code >= 0).astype(jnp.int32)
            return count

        count = lax.fori_loop(0, peers, peer_loop, 0)
        for extra in range(UNROLL):
            listed[number, count + extra] = -1
        return lax.div(count + UNROLL - 1, UNROLL)

    rounds = [list_up(number) for number in range(sub_local)]

    def entry(number, index):
        value = listed[number, index]
        code = jnp.maximum(value, 0)
        peer, rest = parted(code, win_local * tiles * tiles)
        window, spot = parted(rest, tiles * tiles)
        row, column = parted(spot, tiles)
        return value >= 0, peer, window, row, column

    def embed_all(number):
        field[...] = jnp.zeros(field.shape, field.dtype)

        def body(turn, carry):
            todo = []
            for extra in range(UNROLL):
                valid, peer, window, row, column = entry(number, turn * UNROLL + extra)
                at, odd = parted(window, 2)
                lanes = pl.ds(pl.multiple_of(at * pair, pair), pair)
                at, column_odd = parted(column, 2)
                target = pl.ds(pl.multiple_of(at * pair, pair), pair)
                chosen = lane_half == jnp.where(valid, column_odd, 2)
                shift = (odd ^ column_odd) * win
                for part in range(2):
                    piece = strips_ref[peer, part, :, lanes].astype(jnp.float32)
                    piece = jnp.where(chosen, pltpu.roll(piece, shift, 1), 0.0)
                    rows = pl.ds(pl.multiple_of(part * size + row * win, win), win)
                    todo.append((rows, target, piece))
            for rows, target, piece in todo:
                field[rows, target] += piece
            return carry

        lax.fori_loop(0, rounds[number], body, 0)
        tall_all[number] = field[...].astype(jnp.bfloat16)

    for copy in loads:
        copy.wait()
    for number in range(sub_local):
        embed_all(number)
    for copy in tables:
        copy.wait()

    def transform(number, carry):
        tall = tall_all.at[number]

        def left(table_ref):
            for part in range(2):
                for half in range(size // step):
                    rows = pl.ds(part * size + half * step, step)
                    flat[pl.ds(half * step, step), pl.ds(part * size, size)] = jnp.dot(
                        table_ref[rows, :], tall[...], preferred_element_type=jnp.float32
                    ).astype(jnp.bfloat16)

        def right(table_ref, screen_ref):
            for half in range(size // step):
                rows = pl.ds(half * step, step)
                product = jnp.dot(flat[rows, :], table_ref[...], preferred_element_type=jnp.float32)
                real_part, imag_part = product[:, :size], product[:, size:]
                screen_real = screen_ref[0, rows, :].astype(jnp.float32)
                screen_imag = screen_ref[1, rows, :].astype(jnp.float32)
                tall[rows, :] = (real_part * screen_real - imag_part * screen_imag).astype(
                    jnp.bfloat16
                )
                tall[pl.ds(size + half * step, step), :] = (
                    real_part * screen_imag + imag_part * screen_real
                ).astype(jnp.bfloat16)

        left(first_ref)
        right(forward_ref, screen_first_ref)
        left(forward_ref)
        right(inverse_ref, screen_second_ref)
        return carry

    lax.fori_loop(0, sub_local, transform, 0)

    def cut_all(number):
        def body(turn, carry):
            todo = []
            for extra in range(UNROLL):
                valid, peer, window, row, column = entry(number, turn * UNROLL + extra)
                at, column_odd = parted(column, 2)
                source = pl.ds(pl.multiple_of(at * pair, pair), pair)
                part_index, spot = parted(window, part_windows)
                at, odd = parted(spot, 2)
                lanes = pl.ds(pl.multiple_of(at * pair, pair), pair)
                outer, inner = parted(part_index, 2)
                slab = (inner * peers + peer) * (parts // 2) + outer
                chosen = lane_half == jnp.where(valid, odd, 2)
                shift = (odd ^ column_odd) * win
                for part in range(2):
                    rows = pl.ds(pl.multiple_of(part * size + row * win, win), win)
                    piece = tall_all[number, rows, source].astype(jnp.float32)
                    piece = jnp.where(chosen, pltpu.roll(piece, shift, 1), 0.0)
                    todo.append((slab, part, lanes, piece))
            for slab, part, lanes, piece in todo:
                held = out_ref[slab, part, :, lanes].astype(jnp.float32)
                out_ref[slab, part, :, lanes] = (held + piece).astype(out_ref.dtype)
            return carry

        lax.fori_loop(0, rounds[number], body, 0)

    for number in range(sub_local):
        cut_all(number)
    copy = pltpu.make_async_copy(out_ref, out_hbm, out_sem)
    copy.start()
    copy.wait()


def entry_codes(owners, live, place, subgrid_count, tile_count):
    win_local = owners.shape[1]
    capacity = max(2, (7 * win_local + 2 * subgrid_count - 1) // (2 * subgrid_count))
    joined = jnp.where(live[0] == 1, owners[0] * tile_count + place[0], -1).reshape(-1)
    owner = jnp.floor_divide(joined, tile_count)
    count = joined.shape[0]
    window = jnp.arange(count, dtype=jnp.int32) // 3
    label = window * tile_count + (joined - owner * tile_count) + 1
    order = jnp.arange(count, dtype=jnp.int32)
    earlier = (owner[:, None] == owner[None, :]) & (order[None, :] < order[:, None])
    rank = jnp.sum(earlier.astype(jnp.int32), axis=1)
    slot = jnp.where(joined >= 0, owner * capacity + rank, -1)
    slots = jnp.arange(subgrid_count * capacity, dtype=jnp.int32)
    hit = slot[None, :] == slots[:, None]
    codes = jnp.sum(jnp.where(hit, label[None, :], 0), axis=1) - 1
    return codes.reshape(subgrid_count, capacity)


def gathered(strip, screen_first, screen_second, owners, live, place):
    win_size = strip.shape[1]
    sub_size = screen_first.shape[-1]
    tile_count = (sub_size // win_size) ** 2
    peer_count = lax.axis_size("facet")
    parts = lax.axis_size("col")
    sub_local = SUB_DEV
    codes = entry_codes(owners, live, place, sub_local * peer_count, tile_count)
    capacity = codes.shape[1]
    strips, codes, first, forward, inverse = gather_strips(
        strip, codes, peer_count, sub_size, win_size
    )
    piece = strip.shape[2] // parts
    anywhere = pl.BlockSpec(memory_space=pl.ANY)
    slabs = (peer_count * parts, 2, win_size, piece)
    listing = -(-(peer_count * capacity + UNROLL) // 128) * 128
    partial = pl.pallas_call(
        functools.partial(local_body, sub_local, capacity),
        out_shape=jax.ShapeDtypeStruct(slabs, jnp.bfloat16),
        in_specs=[pl.BlockSpec(memory_space=pltpu.SMEM)] + [anywhere] * 6,
        out_specs=anywhere,
        scratch_shapes=[
            pltpu.VMEM(array.shape, array.dtype)
            for array in (strips, screen_first, screen_second, first, forward, inverse)
        ]
        + [
            pltpu.VMEM(slabs, jnp.bfloat16),
            pltpu.VMEM((2 * sub_size, sub_size), jnp.float32),
            pltpu.VMEM((sub_local, 2 * sub_size, sub_size), jnp.bfloat16),
            pltpu.VMEM((sub_size, 2 * sub_size), jnp.bfloat16),
            pltpu.SMEM((sub_local, listing), jnp.int32),
            pltpu.SemaphoreType.DMA((peer_count,)),
            pltpu.SemaphoreType.DMA((5,)),
            pltpu.SemaphoreType.DMA,
        ],
        compiler_params=pltpu.CompilerParams(vmem_limit_bytes=60 << 20),
        name="local",
    )(codes, strips, screen_first, screen_second, first, forward, inverse)
    mine = reduce_partials(partial, peer_count // 2, win_size, piece)
    return finish(mine.reshape(2 * win_size, piece), win_size)


def finish(mine, win_size):
    real, imag = host_table(win_size)
    table = jnp.asarray(left_block(real, -imag).astype(np.float32))
    image = jnp.dot(table, mine, precision=lax.Precision.HIGHEST)
    return image.reshape(2, win_size, mine.shape[1])


def shards(strip, screen_first, screen_second, owners, live, place):
    paired = lax.axis_size("facet") % 2 == 0 and lax.axis_size("col") == 4
    if paired and strip.size * strip.dtype.itemsize * lax.axis_size("facet") <= GATHER_BYTES:
        return gathered(strip, screen_first, screen_second, owners, live, place)
    return exchanged(strip, screen_first, screen_second, owners, live, place)


def solution(mesh):
    placed = (
        P(None, None, "facet"),
        P(),
        P(),
        P("col", "facet", None),
        P("col", "facet", None),
        P("col", "facet", None),
    )
    return jax.shard_map(
        shards,
        mesh=mesh,
        in_specs=placed,
        out_specs=P(None, None, ("facet", "col")),
        check_vma=False,
    )
```
